512 devices in a mesh: line: 16 (over y, core), cross: 32 (over z, x).
Axes of the slice: x: 4, y: 8, z: 8, core: 2. Of those that a mesh axis runs over, the one named last changes fastest.
Arguments:
- jacobian: float32 [5, 5, 512, 4096], P(None, None, 'line', 'cross'), may hold values from -41 to 121, as said below
- time_step: float32 [512, 4096], P('line', 'cross'), may hold values from 2 to 8
- source: bfloat16 [5, 512, 4096], P(None, 'line', 'cross'), may hold values from -12 to 15
- cross_flux: bfloat16 [5, 512, 4096], P(None, 'line', 'cross'), may hold values from -12 to 12
Outputs:
- update: float32 [5, 512, 4096], P(None, 'line', 'cross')
The draws below stay inside these ranges and needn't reach their ends.
Inputs may be any that keep to these rules, and one draw needn't show every extreme that they name: Every 5 x 5 block of jacobian is symmetric, and for every line the system matrix of the last step has a positive definite symmetric part.
All inputs are finite; a program needn't handle non-finite values.
Results may differ from the reference program's by a relative error of at most 0.0003.
Values may be sent and summed in bfloat16 or wider, within the bound.
No kernel may reach another device: no remote copies, remote signals or barrier semaphores. Data moves between devices by JAX's collectives and lax.ppermute only.
A program may use at most 64 MiB of HBM per device.

```python
import math
import jax
import jax.numpy as jnp
from jax import lax

NZ = 8
NX = 512
LINES = 4096


drift_period = 512.0


drift_height = 4.0


def draw_jacobian(key, part):
    key_scale, key_mean, key_cell, key_phase, key_drift = jax.random.split(key, 5)
    line_scale = jnp.exp(jax.random.uniform(key_scale, (LINES,), jnp.float32, math.log(8.0), math.log(32.0)))
    base_matrix = jax.random.uniform(key_mean, (5, 5, LINES), jnp.float32, -1.0, 1.0)
    unit_matrix = jnp.eye(5, dtype=jnp.float32)[:, :, None]
    mean_part = line_scale * (2.0 * unit_matrix + 0.5 * (base_matrix + jnp.swapaxes(base_matrix, 0, 1)))
    drift_raw = jax.random.uniform(key_drift, (5, 5, LINES), jnp.float32, -1.0, 1.0)
    drift_matrix = 0.5 * unit_matrix + 0.05 * (drift_raw + jnp.swapaxes(drift_raw, 0, 1))
    phase = jax.random.uniform(key_phase, (LINES,), jnp.float32, 0.0, 2.0 * math.pi)
    position = jnp.arange(NX).astype(jnp.float32)[:, None]
    profile = drift_height * jnp.sin(2.0 * math.pi * position / drift_period + phase[None, :])
    cell_part = jax.random.uniform(key_cell, (5, 5, NX, LINES), jnp.float32, -1.0, 1.0)
    cell_part = 0.005 * (cell_part + jnp.swapaxes(cell_part, 0, 1))
    return mean_part[:, :, None, :] + profile[None, None, :, :] * drift_matrix[:, :, None, :] + cell_part


def draw_source(key, part):
    rough_part = jnp.clip(jax.random.normal(key, (5, NX, LINES), jnp.float32), -4.0, 4.0)
    values = 3.0 * rough_part
    return values.astype(jnp.bfloat16)


def levels(key, extent, cuts, least, top_value):
    def one(axis_at, parts):
        heights = jax.random.uniform(jax.random.fold_in(jax.random.fold_in(key, 6), axis_at), (parts,), jnp.float32, least / len(cuts), top_value / len(cuts))
        return jnp.repeat(jnp.exp(heights), extent[axis_at] // parts).reshape((-1,) + (1,) * (len(extent) - axis_at - 1))

    factor_of = one(*cuts[0])
    for cut in cuts[1:]:
        factor_of = factor_of * one(*cut)
    return factor_of


def gaussian(own_key, dims, width, most, shards=(), kind=jnp.bfloat16):
    values = width * jax.random.normal(own_key, dims, jnp.float32)
    if shards:
        values = values * levels(own_key, dims, shards, -0.22, 0.18)
    return jnp.clip(values, -most, most).astype(kind)


def setup_inputs(seed: int = 0) -> dict:
    splits = jax.random.split(jax.random.key(seed), 5)
    return {
        "jacobian": draw_jacobian(jax.random.fold_in(splits[4], 71), 0),
        "time_step": jnp.clip(jnp.exp(math.log(8.0) - 1.3862944 * jax.random.uniform(splits[1], (NX, LINES), jnp.float32) ** levels(splits[1], (NX, LINES), ((0, 16), (1, 32)), -0.2, 0.2)), 2.0, 8.0),
        "source": draw_source(jax.random.fold_in(splits[4], 71), 0),
        "cross_flux": gaussian(splits[3], (5, NX, LINES), 3.0, 12.0, ((1, 16), (2, 32))),
    }


damping = 0.05


def product(matrix, operand):
    summed = matrix[:, 0][:, None] * operand[0][None]
    for column_index in range(1, matrix.shape[1]):
        summed = summed + matrix[:, column_index][:, None] * operand[column_index][None]
    return summed


def times_vector(matrix, vector):
    return product(matrix, vector[:, None])[:, 0]


def eliminate(matrix, columns):
    unknowns = matrix.shape[0]
    current = jnp.concatenate([matrix, columns], axis=1)
    for column_index in range(unknowns):
        chosen_row = current[column_index]
        pivot_row = chosen_row / chosen_row[column_index][None]
        column_values = current[:, column_index]
        current = current - column_values[:, None] * pivot_row[None]
        current = jnp.concatenate([current[:column_index], pivot_row[None], current[column_index + 1:]], axis=0)
    return current[:, unknowns:]


def reference(jacobian, time_step, source, cross_flux):
    flux_values = cross_flux.astype(jnp.float32)
    padded = jnp.pad(flux_values, ((0, 0), (0, 0), (NZ, NZ)))
    residual = source.astype(jnp.float32) - 0.5 * (padded[:, :, 2 * NZ:] - padded[:, :, :LINES])
    block_width = math.gcd(LINES, 512)
    blocks = LINES // block_width
    unit_matrix = jnp.eye(5, dtype=jnp.float32)[:, :, None]
    inside = jnp.arange(NX)
    has_lower = (inside > 0).astype(jnp.float32)[:, None, None, None]
    has_upper = (inside < NX - 1).astype(jnp.float32)[:, None, None, None]

    def solve_block(number):
        offset = (number * block_width).astype(jnp.int32)
        jac_block = lax.dynamic_slice_in_dim(jacobian, offset, block_width, 3)
        step_part = lax.dynamic_slice_in_dim(time_step, offset, block_width, 1)
        rhs_part = lax.dynamic_slice_in_dim(residual, offset, block_width, 2)
        jac_seq = jnp.moveaxis(jac_block, 2, 0)
        previous = jnp.concatenate([jnp.zeros_like(jac_seq[:1]), jac_seq[:-1]], axis=0)
        following = jnp.concatenate([jac_seq[1:], jnp.zeros_like(jac_seq[:1])], axis=0)
        lower_seq = has_lower * (-previous * 0.5 - damping * unit_matrix)
        upper_seq = has_upper * (following * 0.5 - damping * unit_matrix)
        diagonal_seq = 1.0 / step_part + 2.0 * damping
        rhs_seq = jnp.moveaxis(rhs_part, 1, 0)

        def forward(running, items):
            coupling, reduced = running
            lower_block, upper_block, diagonal, right_side = items
            pivot_block = diagonal * unit_matrix - product(lower_block, coupling)
            source_term = right_side - times_vector(lower_block, reduced)
            solved = eliminate(pivot_block, jnp.concatenate([upper_block, source_term[:, None]], axis=1))
            result = (solved[:, :5], solved[:, 5])
            return result, result

        initial = (jnp.zeros((5, 5, block_width), jnp.float32), jnp.zeros((5, block_width), jnp.float32))
        couplings, reduced_all = lax.scan(forward, initial, (lower_seq, upper_seq, diagonal_seq, rhs_seq))[1]

        def backward(following_value, items):
            coupling, reduced = items
            value = reduced - times_vector(coupling, following_value)
            return value, value

        values = lax.scan(backward, jnp.zeros((5, block_width), jnp.float32), (couplings, reduced_all), reverse=True)[1]
        return jnp.moveaxis(values, 0, 1)

    solved_blocks = lax.map(solve_block, jnp.arange(blocks, dtype=jnp.int32))
    return jnp.moveaxis(solved_blocks, 0, 2).reshape(5, NX, LINES)
```

```python
import jax
import jax.numpy as jnp
from jax import lax
from jax.experimental import pallas as pl
from jax.experimental.pallas import tpu as pltpu
from jax.sharding import PartitionSpec as P

NZ = 8
damping = 0.05

CHUNKS = 8
CELLS = 4
LANES = 128
SENT = 125
ROWS = 128
INV, LOW, UPP, VLOW, VUPP = (25 * k for k in range(5))
STAGE = 125
N = range(5)


def tile(ref, number):
    return ref[8 * number : 8 * number + 8, :]


def block(ref, base):
    return [[tile(ref, base + 5 * a + b) for b in N] for a in N]


def vector(ref, base):
    return [tile(ref, base + a) for a in N]


def keep(ref, base, matrix):
    for a in N:
        for b in N:
            ref[8 * (base + 5 * a + b) : 8 * (base + 5 * a + b) + 8, :] = matrix[a][b]


def keep_vector(ref, base, values):
    for a in N:
        ref[8 * (base + a) : 8 * (base + a) + 8, :] = values[a]


def total(terms):
    result = terms[0]
    for term in terms[1:]:
        result = result + term
    return result


def mm(left, right):
    return [[total([left[a][k] * right[k][b] for k in N]) for b in N] for a in N]


def mv(left, right):
    return [total([left[a][k] * right[k] for k in N]) for a in N]


def plus(left, right):
    return [[left[a][b] + right[a][b] for b in N] for a in N]


def minus(left, right):
    return [[left[a][b] - right[a][b] for b in N] for a in N]


def negative(matrix):
    return [[-matrix[a][b] for b in N] for a in N]


def vplus(left, right):
    return [left[a] + right[a] for a in N]


def vminus(left, right):
    return [left[a] - right[a] for a in N]


def scaled(factor, matrix):
    return [[factor * matrix[a][b] for b in N] for a in N]


def shifted(matrix, amount):
    return [[matrix[a][b] + amount if a == b else matrix[a][b] for b in N] for a in N]


def turn(value, count):
    return pltpu.roll(value, count % CHUNKS, axis=0)


def flipped(matrix):
    return [[matrix[b][a] for b in N] for a in N]


def mturn(matrix, count):
    return [[turn(matrix[a][b], count) for b in N] for a in N]


def vturn(values, count):
    return [turn(values[a], count) for a in N]


def inverse(matrix):
    m = [list(row) for row in matrix]
    for k in N:
        pivot = 1.0 / m[k][k]
        for b in N:
            m[k][b] = pivot if b == k else m[k][b] * pivot
        for a in N:
            if a != k:
                factor = m[a][k]
                for b in N:
                    m[a][b] = -factor * pivot if b == k else m[a][b] - factor * m[k][b]
    return m


def inverse_and_solved(matrix, *sides):
    m = [list(row) + [side[a][b] for side in sides for b in N] for a, row in enumerate(matrix)]
    width = len(m[0])
    for k in N:
        pivot = 1.0 / m[k][k]
        for b in range(width):
            m[k][b] = pivot if b == k else m[k][b] * pivot
        for a in N:
            if a != k:
                factor = m[a][k]
                for b in range(width):
                    m[a][b] = -factor * pivot if b == k else m[a][b] - factor * m[k][b]
    return [[row[at : at + 5] for row in m] for at in range(0, width, 5)]


def half_jacobian(jac_ref, cell):
    half = [[None] * 5 for _ in N]
    for a in N:
        for b in range(a, 5):
            half[a][b] = half[b][a] = 0.5 * jac_ref[a, b, pl.ds(cell, CHUNKS, stride=CELLS), :]
    return half


def half_before(half_last):
    first = lax.broadcasted_iota(jnp.int32, (CHUNKS, LANES), 0) == 0
    result = [[None] * 5 for _ in N]
    for a in N:
        for b in range(a, 5):
            outside = 1.0 - damping if a == b else 0.0
            result[a][b] = result[b][a] = jnp.where(first, outside, turn(half_last[a][b], 1))
    return result


def diagonal(step_ref, cell):
    return 1.0 / step_ref[pl.ds(cell, CHUNKS, stride=CELLS), :] + 2.0 * damping


def stage(fac_ref, base, low, own, nxt, upp, distance):
    inv = inverse(plus(own, nxt))
    vlow = mm(inv, low)
    vupp = mm(inv, upp)
    keep(fac_ref, base + INV, inv)
    keep(fac_ref, base + LOW, low)
    keep(fac_ref, base + UPP, upp)
    keep(fac_ref, base + VLOW, vlow)
    keep(fac_ref, base + VUPP, vupp)
    own = minus(own, mm(low, mturn(vupp, distance)))
    nxt = minus(nxt, mm(upp, mturn(vlow, -distance)))
    low = negative(mm(low, mturn(vlow, distance)))
    upp = negative(mm(upp, mturn(vupp, -distance)))
    return low, own, nxt, upp


def stage_rhs(fac_ref, base, own, nxt, distance):
    value = mv(block(fac_ref, base + INV), vplus(own, nxt))
    own = vminus(own, mv(block(fac_ref, base + LOW), vturn(value, distance)))
    nxt = vminus(nxt, mv(block(fac_ref, base + UPP), vturn(value, -distance)))
    return value, own, nxt


def stage_back(fac_ref, base, value, before, after):
    return vminus(
        vminus(value, mv(block(fac_ref, base + VLOW), before)), mv(block(fac_ref, base + VUPP), after)
    )


def rows_of_last(ref, group):
    return ref[pl.ds(64 * group + 7, 8, stride=8), :]


def merge(fac_ref, base, former, latter, upp, low):
    head_head, head_tail, tail_head, tail_tail = former
    inv_head, carry, reach = inverse_and_solved(latter[0], low, latter[1])
    inv_tail, tail_by_head, tail_by_tail = inverse_and_solved(
        plus(tail_tail, mm(upp, carry)), tail_head, mm(upp, reach)
    )
    head_by_head = mm(carry, tail_by_head)
    head_by_tail = minus(reach, mm(carry, tail_by_tail))
    for number, kept in enumerate(
        (
            inv_head,
            carry,
            inv_tail,
            upp,
            head_tail,
            latter[2],
            tail_by_head,
            tail_by_tail,
            head_by_head,
            head_by_tail,
        )
    ):
        keep(fac_ref, base + 25 * number, kept)
    return (
        minus(head_head, mm(head_tail, tail_by_head)),
        mm(head_tail, tail_by_tail),
        negative(mm(latter[2], head_by_head)),
        minus(latter[3], mm(latter[2], head_by_tail)),
    )


def merge_rhs(fac_ref, base, former, latter):
    head = mv(block(fac_ref, base), latter[0])
    tail = mv(block(fac_ref, base + 50), vminus(former[1], mv(block(fac_ref, base + 75), head)))
    head = vplus(head, mv(block(fac_ref, base + 25), tail))
    return (
        tail,
        head,
        vminus(former[0], mv(block(fac_ref, base + 100), tail)),
        vminus(latter[1], mv(block(fac_ref, base + 125), head)),
    )


def merge_back(fac_ref, base, tail, head, first, last):
    tail = vplus(
        vminus(tail, mv(block(fac_ref, base + 150), first)), mv(block(fac_ref, base + 175), last)
    )
    head = vminus(
        vminus(head, mv(block(fac_ref, base + 200), first)), mv(block(fac_ref, base + 225), last)
    )
    return tail, head


def rows_of_first(ref, group):
    return ref[pl.ds(64 * group, 8, stride=8), :]


MERGES = ((1, 200), (2, 450), (4, 700))
CLOSE = 950
TILES = 1050


def factor_kernel(jac_ref, step_ref, fac_ref, pack_ref, end_ref):
    e = damping
    h0 = half_jacobian(jac_ref, 0)
    h1 = half_jacobian(jac_ref, 1)
    h2 = half_jacobian(jac_ref, 2)
    h3 = half_jacobian(jac_ref, 3)
    d1 = diagonal(step_ref, 1)
    d2 = diagonal(step_ref, 2)
    h0p, h1p, h2p, h3p = shifted(h0, e), shifted(h1, e), shifted(h2, e), shifted(h3, e)
    h0m, h1m, h2m, h3m = shifted(h0, -e), shifted(h1, -e), shifted(h2, -e), shifted(h3, -e)
    inv = inverse(shifted(mm(h2m, h1p), d1 * d2))
    by_low = mm(inv, h0p)
    by_upp = mm(inv, mm(h2m, h3m))
    by_end = mm(flipped(inv), h3m)
    pair = mm(h2p, h1p)
    group = (
        shifted(mm(h1m, scaled(d2, by_low)), diagonal(step_ref, 0)),
        mm(h1m, by_upp),
        negative(mm(pair, by_low)),
        shifted(mm(scaled(d1, h2p), by_end), diagonal(step_ref, 3)),
    )
    keep(fac_ref, 0, inv)
    keep(fac_ref, 25, by_low)
    keep(fac_ref, 50, by_upp)
    keep(fac_ref, 75, by_end)
    for distance, base in MERGES:
        latter = tuple(mturn(part, -distance) for part in group)
        group = merge(fac_ref, base, group, latter, mturn(h0m, -distance), mturn(h3p, 1 - distance))
    head_head, head_tail, tail_head, tail_tail = group
    inv = inverse(head_head)
    reach = mm(inv, head_tail)
    through = mm(tail_head, inv)
    into = mm(h0m, inv)
    keep(fac_ref, CLOSE, inv)
    keep(fac_ref, CLOSE + 25, reach)
    keep(fac_ref, CLOSE + 50, through)
    keep(fac_ref, CLOSE + 75, into)
    keep(end_ref, 0, through)
    keep(end_ref, 25, minus(tail_tail, mm(tail_head, reach)))
    keep(end_ref, 50, into)
    keep(end_ref, 75, negative(mm(h0m, reach)))
    place = 100
    for a in N:
        for b in range(a, 5):
            end_ref[8 * place : 8 * place + 8, :] = turn(h3p[a][b], 1)
            place += 1
    for number in range(15):
        pack_ref[8 * number : 8 * number + 8, :] = rows_of_first(end_ref, number)


def rhs_kernel(
    jac_ref, step_ref, src_ref, flux_ref, before_ref, after_ref, fac_ref, part_ref, pack_ref, val_ref, res_ref, end_ref
):
    e = damping
    lane = lax.broadcasted_iota(jnp.int32, (CHUNKS * CELLS, LANES), 1)
    for a in N:
        flux = flux_ref[a].astype(jnp.float32)
        upper = pltpu.roll(jnp.where(lane < NZ, after_ref[a].astype(jnp.float32), flux), LANES - NZ, axis=1)
        lower = pltpu.roll(jnp.where(lane >= LANES - NZ, before_ref[a].astype(jnp.float32), flux), NZ, axis=1)
        res_ref[a] = src_ref[a].astype(jnp.float32) - 0.5 * (upper - lower)
    r0, r1, r2, r3 = ([res_ref[a, pl.ds(cell, CHUNKS, stride=CELLS), :] for a in N] for cell in range(CELLS))
    h1 = half_jacobian(jac_ref, 1)
    h2 = half_jacobian(jac_ref, 2)
    d1 = diagonal(step_ref, 1)
    d2 = diagonal(step_ref, 2)
    inv = block(fac_ref, 0)
    part = mv(inv, r1)
    x1 = vminus([d2 * value for value in part], mv(inv, mv(shifted(h2, -e), r2)))
    x2 = vplus(mv(shifted(h1, e), part), [d1 * value for value in mv(flipped(inv), r2)])
    keep_vector(val_ref, 0, x1)
    keep_vector(val_ref, 5, x2)
    head = vminus(r0, mv(shifted(h1, -e), x1))
    tail = vplus(r3, mv(shifted(h2, e), x2))
    place = 10
    for distance, base in MERGES:
        latter = (vturn(head, -distance), vturn(tail, -distance))
        inner_tail, inner_head, head, tail = merge_rhs(fac_ref, base, (head, tail), latter)
        keep_vector(val_ref, place, inner_tail)
        keep_vector(val_ref, place + 5, inner_head)
        place += 10
    keep_vector(val_ref, place, mv(block(fac_ref, CLOSE), head))
    end_ref[...] = jnp.zeros_like(end_ref)
    keep_vector(end_ref, 3, vminus(tail, mv(block(fac_ref, CLOSE + 50), head)))
    keep_vector(end_ref, 8, [-value for value in mv(block(fac_ref, CLOSE + 75), head)])
    pack_ref[:112, :] = part_ref[:112, :]
    row = lax.broadcasted_iota(jnp.int32, (8, LANES), 0)
    pack_ref[112:120, :] = jnp.where(row < 3, part_ref[112:120, :], rows_of_first(end_ref, 0))
    pack_ref[120:125, :] = rows_of_first(end_ref, 1)[:5]


def solve_kernel(sent_ref, jac_ref, step_ref, fac_ref, val_ref, out_ref, all_ref, red_ref, x_ref, w_ref):
    e = damping
    for device in range(16):
        all_ref[ROWS * device : ROWS * device + SENT, :] = sent_ref[device]
    row = lax.broadcasted_iota(jnp.int32, (CHUNKS, LANES), 0)

    def packed(parity, number):
        return all_ref[pl.ds(parity * ROWS + number, 8, stride=2 * ROWS), :]

    def packed_block(parity, base):
        return [[packed(parity, base + 5 * a + b) for b in N] for a in N]

    def packed_vector(parity, base):
        return [packed(parity, base + a) for a in N]

    def packed_symmetric(parity, base):
        result = [[None] * 5 for _ in N]
        for a in N:
            for b in range(a, 5):
                result[a][b] = result[b][a] = packed(parity, base)
                base += 1
        return result

    m_even = packed_symmetric(0, 100)
    m_odd = packed_symmetric(1, 100)
    inv = inverse(plus(packed_block(0, 25), mm(packed_block(1, 50), m_even)))
    vlow = mm(inv, packed_block(0, 0))
    vupp = mm(inv, packed_block(1, 75))
    value = mv(inv, vplus(packed_vector(0, 115), packed_vector(1, 120)))
    keep(red_ref, VLOW, vlow)
    keep(red_ref, VUPP, vupp)
    keep_vector(x_ref, 4, value)
    cross = mm(packed_block(1, 0), m_even)
    own = minus(packed_block(1, 25), mm(cross, vupp))
    low = negative(mm(cross, vlow))
    own_rhs = vminus(packed_vector(1, 115), mv(cross, value))
    back = packed_block(0, 75)
    nxt = minus(packed_block(0, 50), mm(back, vlow))
    upp = negative(mm(back, vupp))
    nxt_rhs = vminus(packed_vector(0, 120), mv(back, value))
    first, last = row == 0, row == CHUNKS - 1
    low = mm(low, mturn(m_odd, 1))
    low = [[jnp.where(first, 0.0, low[a][b]) for b in N] for a in N]
    nxt = mm(mturn(nxt, -1), m_odd)
    nxt = [[jnp.where(last, 0.0, nxt[a][b]) for b in N] for a in N]
    upp = [[jnp.where(last, 0.0, turn(upp[a][b], -1)) for b in N] for a in N]
    nxt_rhs = [jnp.where(last, 0.0, turn(nxt_rhs[a], -1)) for a in N]
    levels = ((1, 1), (2, 2), (3, 4))
    values = []
    for number, distance in levels:
        low, own, nxt, upp = stage(red_ref, number * STAGE, low, own, nxt, upp, distance)
        value, own_rhs, nxt_rhs = stage_rhs(red_ref, number * STAGE, own_rhs, nxt_rhs, distance)
        values.append(value)
    x = mv(inverse(plus(own, nxt)), vplus(own_rhs, nxt_rhs))
    for number, distance in reversed(levels):
        found = stage_back(red_ref, number * STAGE, values[number - 1], vturn(x, distance), vturn(x, -distance))
        chosen = (row % (2 * distance)) == distance - 1
        x = [jnp.where(chosen, found[a], x[a]) for a in N]
    w_odd = mv(m_odd, x)
    before = [jnp.where(first, 0.0, turn(w_odd[a], 1)) for a in N]
    x_even = stage_back(red_ref, 0, vector(x_ref, 4), before, x)
    w_even = mv(m_even, x_even)
    position = lax.axis_index("line")
    half, odd = position // 2, position % 2
    is_odd = odd == 1
    for a in N:
        w_ref[8 * a : 8 * a + 8, :] = jnp.where(is_odd, w_even[a], before[a])
        x_ref[8 * a : 8 * a + 8, :] = jnp.where(is_odd, x[a], x_even[a])
    ends = [jnp.broadcast_to(x_ref[pl.ds(8 * a + half, 1), :], (CHUNKS, LANES)) for a in N]
    w = [jnp.broadcast_to(w_ref[pl.ds(8 * a + half, 1), :], (CHUNKS, LANES)) for a in N]

    last = ends
    first = vplus(vector(val_ref, 40), vminus(mv(block(fac_ref, CLOSE), w), mv(block(fac_ref, CLOSE + 25), last)))
    place = 30
    for distance, base in reversed(MERGES):
        tail, head = merge_back(fac_ref, base, vector(val_ref, place), vector(val_ref, place + 5), first, last)
        place -= 10
        latter = (row % (2 * distance)) >= distance
        first = [jnp.where(latter, turn(head[a], distance), first[a]) for a in N]
        last = [jnp.where(latter, turn(last[a], distance), tail[a]) for a in N]
    d1 = diagonal(step_ref, 1)
    d2 = diagonal(step_ref, 2)
    part = mv(block(fac_ref, 25), first)
    x1 = vplus(vplus(vector(val_ref, 0), [d2 * value for value in part]), mv(block(fac_ref, 50), last))
    far = mv(block(fac_ref, 75), last)
    near = mv(shifted(half_jacobian(jac_ref, 1), e), part)
    x2 = vplus(vector(val_ref, 5), vminus(near, [d1 * value for value in far]))
    for a in N:
        out_ref[a, pl.ds(0, CHUNKS, stride=CELLS), :] = first[a]
        out_ref[a, pl.ds(1, CHUNKS, stride=CELLS), :] = x1[a]
        out_ref[a, pl.ds(2, CHUNKS, stride=CELLS), :] = x2[a]
        out_ref[a, pl.ds(3, CHUNKS, stride=CELLS), :] = last[a]


INTERPRET = False


def run(kernel, name, outs, args, scratch):
    inside = pl.BlockSpec(memory_space=pltpu.VMEM)
    if INTERPRET:
        shapes = [jax.ShapeDtypeStruct(shape, jnp.float32) for shape in outs]
    else:
        args = [pltpu.with_memory_space_constraint(arg, pltpu.VMEM) for arg in args]
        shapes = [pltpu.VMEM(shape, jnp.float32) for shape in outs]
    return pl.pallas_call(
        kernel,
        out_shape=shapes,
        in_specs=[inside] * len(args),
        out_specs=[inside] * len(outs),
        scratch_shapes=[pltpu.VMEM(shape, jnp.float32) for shape in scratch],
        interpret=INTERPRET,
        compiler_params=pltpu.CompilerParams(vmem_limit_bytes=12 << 20),
        name=name,
    )(*args)


def shards(jacobian, time_step, source, cross_flux):
    count = lax.axis_size("cross")
    before = lax.ppermute(cross_flux, "cross", [(i, i + 1) for i in range(count - 1)])
    after = lax.ppermute(cross_flux, "cross", [(i + 1, i) for i in range(count - 1)])
    factors, part = run(
        factor_kernel, "factor", [(TILES * 8, LANES), (120, LANES)], [jacobian, time_step], [(120 * 8, LANES)]
    )
    packet, values = run(
        rhs_kernel,
        "right_side",
        [(SENT, LANES), (45 * 8, LANES)],
        [jacobian, time_step, source, cross_flux, before, after, factors, part],
        [(5, CHUNKS * CELLS, LANES), (16 * 8, LANES)],
    )
    packets = lax.all_gather(packet, "line", axis=0)
    return run(
        solve_kernel,
        "solve",
        [(5, CHUNKS * CELLS, LANES)],
        [packets, jacobian, time_step, factors, values],
        [(16 * ROWS, LANES), (4 * STAGE * 8, LANES), (16 * 8, LANES), (5 * 8, LANES)],
    )[0]


def solution(mesh):
    placed = (
        P(None, None, "line", "cross"),
        P("line", "cross"),
        P(None, "line", "cross"),
        P(None, "line", "cross"),
    )
    return jax.shard_map(
        shards, mesh=mesh, in_specs=placed, out_specs=P(None, "line", "cross"), check_vma=False
    )
```

```python
import jax
import jax.numpy as jnp
from jax import lax
from jax.experimental import pallas as pl
from jax.experimental.pallas import tpu as pltpu
from jax.sharding import PartitionSpec as P

NZ = 8
damping = 0.05

CHUNKS = 8
CELLS = 4
LANES = 128
SENT = 125
ROWS = 128
INV, LOW, UPP, VLOW, VUPP = (25 * k for k in range(5))
STAGE = 125
N = range(5)


def tile(ref, number):
    return ref[8 * number : 8 * number + 8, :]


def block(ref, base):
    return [[tile(ref, base + 5 * a + b) for b in N] for a in N]


def vector(ref, base):
    return [tile(ref, base + a) for a in N]


def keep(ref, base, matrix):
    for a in N:
        for b in N:
            ref[8 * (base + 5 * a + b) : 8 * (base + 5 * a + b) + 8, :] = matrix[a][b]


def keep_vector(ref, base, values):
    for a in N:
        ref[8 * (base + a) : 8 * (base + a) + 8, :] = values[a]


def total(terms):
    result = terms[0]
    for term in terms[1:]:
        result = result + term
    return result


def mm(left, right):
    return [[total([left[a][k] * right[k][b] for k in N]) for b in N] for a in N]


def mv(left, right):
    return [total([left[a][k] * right[k] for k in N]) for a in N]


def plus(left, right):
    return [[left[a][b] + right[a][b] for b in N] for a in N]


def minus(left, right):
    return [[left[a][b] - right[a][b] for b in N] for a in N]


def negative(matrix):
    return [[-matrix[a][b] for b in N] for a in N]


def vplus(left, right):
    return [left[a] + right[a] for a in N]


def vminus(left, right):
    return [left[a] - right[a] for a in N]


def scaled(factor, matrix):
    return [[factor * matrix[a][b] for b in N] for a in N]


def shifted(matrix, amount):
    return [[matrix[a][b] + amount if a == b else matrix[a][b] for b in N] for a in N]


def turn(value, count):
    return pltpu.roll(value, count % CHUNKS, axis=0)


def flipped(matrix):
    return [[matrix[b][a] for b in N] for a in N]


def mturn(matrix, count):
    return [[turn(matrix[a][b], count) for b in N] for a in N]


def vturn(values, count):
    return [turn(values[a], count) for a in N]


def inverse(matrix):
    m = [list(row) for row in matrix]
    for k in N:
        pivot = 1.0 / m[k][k]
        for b in N:
            m[k][b] = pivot if b == k else m[k][b] * pivot
        for a in N:
            if a != k:
                factor = m[a][k]
                for b in N:
                    m[a][b] = -factor * pivot if b == k else m[a][b] - factor * m[k][b]
    return m


def inverse_and_solved(matrix, *sides):
    m = [list(row) + [side[a][b] for side in sides for b in N] for a, row in enumerate(matrix)]
    width = len(m[0])
    for k in N:
        pivot = 1.0 / m[k][k]
        for b in range(width):
            m[k][b] = pivot if b == k else m[k][b] * pivot
        for a in N:
            if a != k:
                factor = m[a][k]
                for b in range(width):
                    m[a][b] = -factor * pivot if b == k else m[a][b] - factor * m[k][b]
    return [[row[at : at + 5] for row in m] for at in range(0, width, 5)]


def half_jacobian(jac_ref, cell):
    half = [[None] * 5 for _ in N]
    for a in N:
        for b in range(a, 5):
            half[a][b] = half[b][a] = 0.5 * jac_ref[a, b, pl.ds(cell, CHUNKS, stride=CELLS), :]
    return half


def half_before(half_last):
    first = lax.broadcasted_iota(jnp.int32, (CHUNKS, LANES), 0) == 0
    result = [[None] * 5 for _ in N]
    for a in N:
        for b in range(a, 5):
            outside = 1.0 - damping if a == b else 0.0
            result[a][b] = result[b][a] = jnp.where(first, outside, turn(half_last[a][b], 1))
    return result


def diagonal(step_ref, cell):
    return 1.0 / step_ref[pl.ds(cell, CHUNKS, stride=CELLS), :] + 2.0 * damping


def stage(fac_ref, base, low, own, nxt, upp, distance):
    inv, vlow, vupp = inverse_and_solved(plus(own, nxt), low, upp)
    keep(fac_ref, base + INV, inv)
    keep(fac_ref, base + LOW, low)
    keep(fac_ref, base + UPP, upp)
    keep(fac_ref, base + VLOW, vlow)
    keep(fac_ref, base + VUPP, vupp)
    own = minus(own, mm(low, mturn(vupp, distance)))
    nxt = minus(nxt, mm(upp, mturn(vlow, -distance)))
    low = negative(mm(low, mturn(vlow, distance)))
    upp = negative(mm(upp, mturn(vupp, -distance)))
    return low, own, nxt, upp


def stage_rhs(fac_ref, base, own, nxt, distance):
    value = mv(block(fac_ref, base + INV), vplus(own, nxt))
    own = vminus(own, mv(block(fac_ref, base + LOW), vturn(value, distance)))
    nxt = vminus(nxt, mv(block(fac_ref, base + UPP), vturn(value, -distance)))
    return value, own, nxt


def stage_back(fac_ref, base, value, before, after):
    return vminus(
        vminus(value, mv(block(fac_ref, base + VLOW), before)), mv(block(fac_ref, base + VUPP), after)
    )


def merge(fac_ref, base, former, latter, upp, low):
    head_head, head_tail, tail_head, tail_tail = former
    inv_head, carry, reach = inverse_and_solved(latter[0], low, latter[1])
    inv_tail, tail_by_head, tail_by_tail = inverse_and_solved(
        plus(tail_tail, mm(upp, carry)), tail_head, mm(upp, reach)
    )
    head_by_head = mm(carry, tail_by_head)
    head_by_tail = minus(reach, mm(carry, tail_by_tail))
    for number, kept in enumerate(
        (
            inv_head,
            carry,
            inv_tail,
            upp,
            head_tail,
            latter[2],
            tail_by_head,
            tail_by_tail,
            head_by_head,
            head_by_tail,
        )
    ):
        keep(fac_ref, base + 25 * number, kept)
    return (
        minus(head_head, mm(head_tail, tail_by_head)),
        mm(head_tail, tail_by_tail),
        negative(mm(latter[2], head_by_head)),
        minus(latter[3], mm(latter[2], head_by_tail)),
    )


def merge_rhs(fac_ref, base, former, latter):
    head = mv(block(fac_ref, base), latter[0])
    tail = mv(block(fac_ref, base + 50), vminus(former[1], mv(block(fac_ref, base + 75), head)))
    head = vplus(head, mv(block(fac_ref, base + 25), tail))
    return (
        tail,
        head,
        vminus(former[0], mv(block(fac_ref, base + 100), tail)),
        vminus(latter[1], mv(block(fac_ref, base + 125), head)),
    )


def merge_back(fac_ref, base, tail, head, first, last):
    tail = vplus(
        vminus(tail, mv(block(fac_ref, base + 150), first)), mv(block(fac_ref, base + 175), last)
    )
    head = vminus(
        vminus(head, mv(block(fac_ref, base + 200), first)), mv(block(fac_ref, base + 225), last)
    )
    return tail, head


def rows_of_last(ref, group):
    return ref[pl.ds(64 * group + CHUNKS - WIDTH, 8, stride=8), :]


WIDTH = 2
MERGES = tuple((1 << k, 100 + 250 * k) for k in range(WIDTH.bit_length() - 1))
CLOSE = 100 + 250 * len(MERGES)
STAGES = tuple((WIDTH << k, CLOSE + 100 + 125 * k) for k in range((CHUNKS // WIDTH).bit_length() - 1))
TILES = CLOSE + 100 + 125 * len(STAGES)
VALUES = 15 + 10 * len(MERGES) + 5 * len(STAGES)


def factor_kernel(
    jac_hbm, step_hbm, src_hbm, flux_hbm, jac_ref, step_ref, src_ref, flux_ref, fac_ref, pack_ref, end_ref, sems
):
    needed = [pltpu.make_async_copy(jac_hbm.at[a, a:], jac_ref.at[a, a:], sems.at[a]) for a in N]
    needed.append(pltpu.make_async_copy(step_hbm, step_ref, sems.at[5]))
    later = [
        pltpu.make_async_copy(src_hbm, src_ref, sems.at[6]),
        pltpu.make_async_copy(flux_hbm, flux_ref, sems.at[7]),
    ]
    for copy in needed + later:
        copy.start()
    for copy in needed:
        copy.wait()
    factor(jac_ref, step_ref, fac_ref, pack_ref, end_ref)
    for copy in later:
        copy.wait()


def factor(jac_ref, step_ref, fac_ref, pack_ref, end_ref):
    e = damping
    h0 = half_jacobian(jac_ref, 0)
    h1 = half_jacobian(jac_ref, 1)
    h2 = half_jacobian(jac_ref, 2)
    h3 = half_jacobian(jac_ref, 3)
    d1 = diagonal(step_ref, 1)
    d2 = diagonal(step_ref, 2)
    h0p, h1p, h2p, h3p = shifted(h0, e), shifted(h1, e), shifted(h2, e), shifted(h3, e)
    h0m, h1m, h2m, h3m = shifted(h0, -e), shifted(h1, -e), shifted(h2, -e), shifted(h3, -e)
    inv, by_low, by_upp = inverse_and_solved(shifted(mm(h2m, h1p), d1 * d2), h0p, mm(h2m, h3m))
    by_end = mm(flipped(inv), h3m)
    pair = mm(h2p, h1p)
    group = (
        shifted(mm(h1m, scaled(d2, by_low)), diagonal(step_ref, 0)),
        mm(h1m, by_upp),
        negative(mm(pair, by_low)),
        shifted(mm(scaled(d1, h2p), by_end), diagonal(step_ref, 3)),
    )
    keep(fac_ref, 0, inv)
    keep(fac_ref, 25, by_low)
    keep(fac_ref, 50, by_upp)
    keep(fac_ref, 75, by_end)
    for distance, base in MERGES:
        latter = tuple(mturn(part, -distance) for part in group)
        group = merge(fac_ref, base, group, latter, mturn(h0m, -distance), mturn(h3p, 1 - distance))
    head_head, head_tail, tail_head, tail_tail = group
    inv, reach = inverse_and_solved(head_head, head_tail)
    through = mm(tail_head, inv)
    into = mm(h0m, inv)
    keep(fac_ref, CLOSE, inv)
    keep(fac_ref, CLOSE + 25, reach)
    keep(fac_ref, CLOSE + 50, through)
    keep(fac_ref, CLOSE + 75, into)
    own = minus(tail_tail, mm(tail_head, reach))
    upp = mturn(negative(mm(h0m, reach)), -WIDTH)
    low, nxt = through, into
    if STAGES:
        link = shifted(half_before(h3), e)
        low, nxt = mm(through, link), mm(into, link)
    nxt = mturn(nxt, -WIDTH)
    for distance, base in STAGES:
        low, own, nxt, upp = stage(fac_ref, base, low, own, nxt, upp, distance)
    keep(end_ref, 0, low)
    keep(end_ref, 25, own)
    keep(end_ref, 50, nxt)
    keep(end_ref, 75, upp)
    place = 100
    for a in N:
        for b in range(a, 5):
            end_ref[8 * place : 8 * place + 8, :] = turn(h3p[a][b], 1 - WIDTH)
            place += 1
    for number in range(15):
        pack_ref[8 * number : 8 * number + 8, :] = rows_of_last(end_ref, number)


def rhs_kernel(
    jac_ref, step_ref, src_ref, flux_ref, before_ref, after_ref, fac_ref, part_ref, pack_ref, val_ref, res_ref, end_ref
):
    e = damping
    lane = lax.broadcasted_iota(jnp.int32, (CHUNKS * CELLS, LANES), 1)
    for a in N:
        flux = flux_ref[a].astype(jnp.float32)
        upper = pltpu.roll(jnp.where(lane < NZ, after_ref[a].astype(jnp.float32), flux), LANES - NZ, axis=1)
        lower = pltpu.roll(jnp.where(lane >= LANES - NZ, before_ref[a].astype(jnp.float32), flux), NZ, axis=1)
        res_ref[a] = src_ref[a].astype(jnp.float32) - 0.5 * (upper - lower)
    r0, r1, r2, r3 = ([res_ref[a, pl.ds(cell, CHUNKS, stride=CELLS), :] for a in N] for cell in range(CELLS))
    h1 = half_jacobian(jac_ref, 1)
    h2 = half_jacobian(jac_ref, 2)
    d1 = diagonal(step_ref, 1)
    d2 = diagonal(step_ref, 2)
    inv = block(fac_ref, 0)
    part = mv(inv, r1)
    x1 = vminus([d2 * value for value in part], mv(inv, mv(shifted(h2, -e), r2)))
    x2 = vplus(mv(shifted(h1, e), part), [d1 * value for value in mv(flipped(inv), r2)])
    keep_vector(val_ref, 0, x1)
    keep_vector(val_ref, 5, x2)
    head = vminus(r0, mv(shifted(h1, -e), x1))
    tail = vplus(r3, mv(shifted(h2, e), x2))
    place = 10
    for distance, base in MERGES:
        latter = (vturn(head, -distance), vturn(tail, -distance))
        inner_tail, inner_head, head, tail = merge_rhs(fac_ref, base, (head, tail), latter)
        keep_vector(val_ref, place, inner_tail)
        keep_vector(val_ref, place + 5, inner_head)
        place += 10
    keep_vector(val_ref, place, mv(block(fac_ref, CLOSE), head))
    own = vminus(tail, mv(block(fac_ref, CLOSE + 50), head))
    nxt = vturn([-value for value in mv(block(fac_ref, CLOSE + 75), head)], -WIDTH)
    for distance, base in STAGES:
        place += 5
        value, own, nxt = stage_rhs(fac_ref, base, own, nxt, distance)
        keep_vector(val_ref, place, value)
    end_ref[...] = jnp.zeros_like(end_ref)
    keep_vector(end_ref, 3, own)
    keep_vector(end_ref, 8, nxt)
    pack_ref[:112, :] = part_ref[:112, :]
    row = lax.broadcasted_iota(jnp.int32, (8, LANES), 0)
    pack_ref[112:120, :] = jnp.where(row < 3, part_ref[112:120, :], rows_of_last(end_ref, 0))
    pack_ref[120:125, :] = rows_of_last(end_ref, 1)[:5]


def solve_kernel(sent_ref, jac_ref, step_ref, fac_ref, val_ref, out_hbm, out_ref, all_ref, red_ref, x_ref, w_ref, sems):
    solve(sent_ref, jac_ref, step_ref, fac_ref, val_ref, out_ref, all_ref, red_ref, x_ref, w_ref)
    copies = [pltpu.make_async_copy(out_ref.at[a], out_hbm.at[a], sems.at[a]) for a in N]
    for copy in copies:
        copy.start()
    for copy in copies:
        copy.wait()


def solve(sent_ref, jac_ref, step_ref, fac_ref, val_ref, out_ref, all_ref, red_ref, x_ref, w_ref):
    e = damping
    for device in range(16):
        all_ref[ROWS * device : ROWS * device + SENT, :] = sent_ref[device]
    row = lax.broadcasted_iota(jnp.int32, (CHUNKS, LANES), 0)

    def packed(parity, number):
        return all_ref[pl.ds(parity * ROWS + number, 8, stride=2 * ROWS), :]

    def packed_block(parity, base):
        return [[packed(parity, base + 5 * a + b) for b in N] for a in N]

    def packed_vector(parity, base):
        return [packed(parity, base + a) for a in N]

    def packed_symmetric(parity, base):
        result = [[None] * 5 for _ in N]
        for a in N:
            for b in range(a, 5):
                result[a][b] = result[b][a] = packed(parity, base)
                base += 1
        return result

    m_even = packed_symmetric(0, 100)
    m_odd = packed_symmetric(1, 100)
    inv, vlow, vupp = inverse_and_solved(
        plus(packed_block(0, 25), mm(packed_block(1, 50), m_even)), packed_block(0, 0), packed_block(1, 75)
    )
    value = mv(inv, vplus(packed_vector(0, 115), packed_vector(1, 120)))
    keep(red_ref, VLOW, vlow)
    keep(red_ref, VUPP, vupp)
    keep_vector(x_ref, 4, value)
    cross = mm(packed_block(1, 0), m_even)
    own = minus(packed_block(1, 25), mm(cross, vupp))
    low = negative(mm(cross, vlow))
    own_rhs = vminus(packed_vector(1, 115), mv(cross, value))
    back = packed_block(0, 75)
    nxt = minus(packed_block(0, 50), mm(back, vlow))
    upp = negative(mm(back, vupp))
    nxt_rhs = vminus(packed_vector(0, 120), mv(back, value))
    first, last = row == 0, row == CHUNKS - 1
    low = mm(low, mturn(m_odd, 1))
    low = [[jnp.where(first, 0.0, low[a][b]) for b in N] for a in N]
    nxt = mm(mturn(nxt, -1), m_odd)
    nxt = [[jnp.where(last, 0.0, nxt[a][b]) for b in N] for a in N]
    upp = [[jnp.where(last, 0.0, turn(upp[a][b], -1)) for b in N] for a in N]
    nxt_rhs = [jnp.where(last, 0.0, turn(nxt_rhs[a], -1)) for a in N]
    levels = ((1, 1), (2, 2), (3, 4))
    values = []
    for number, distance in levels:
        low, own, nxt, upp = stage(red_ref, number * STAGE, low, own, nxt, upp, distance)
        value, own_rhs, nxt_rhs = stage_rhs(red_ref, number * STAGE, own_rhs, nxt_rhs, distance)
        values.append(value)
    x = mv(inverse(plus(own, nxt)), vplus(own_rhs, nxt_rhs))
    for number, distance in reversed(levels):
        found = stage_back(red_ref, number * STAGE, values[number - 1], vturn(x, distance), vturn(x, -distance))
        chosen = (row % (2 * distance)) == distance - 1
        x = [jnp.where(chosen, found[a], x[a]) for a in N]
    w_odd = mv(m_odd, x)
    before = [jnp.where(first, 0.0, turn(w_odd[a], 1)) for a in N]
    x_even = stage_back(red_ref, 0, vector(x_ref, 4), before, x)
    w_even = mv(m_even, x_even)
    position = lax.axis_index("line")
    half, odd = position // 2, position % 2
    is_odd = odd == 1
    for a in N:
        w_ref[8 * a : 8 * a + 8, :] = jnp.where(is_odd, w_even[a], before[a])
        x_ref[8 * a : 8 * a + 8, :] = jnp.where(is_odd, x[a], x_even[a])
    ends = [jnp.broadcast_to(x_ref[pl.ds(8 * a + half, 1), :], (CHUNKS, LANES)) for a in N]
    w = [jnp.broadcast_to(w_ref[pl.ds(8 * a + half, 1), :], (CHUNKS, LANES)) for a in N]

    def neighbour(values, distance):
        return [jnp.where(row < distance, w[a], turn(values[a], distance)) for a in N]

    last = ends
    place = VALUES - 5
    for distance, base in reversed(STAGES):
        found = stage_back(fac_ref, base, vector(val_ref, place), neighbour(last, distance), vturn(last, -distance))
        place -= 5
        chosen = (row % (2 * distance)) == distance - WIDTH
        last = [jnp.where(chosen, found[a], last[a]) for a in N]
    if STAGES:
        w = mv(shifted(half_before(half_jacobian(jac_ref, 3)), e), neighbour(last, WIDTH))
    first = vplus(
        vector(val_ref, place), vminus(mv(block(fac_ref, CLOSE), w), mv(block(fac_ref, CLOSE + 25), last))
    )
    for distance, base in reversed(MERGES):
        place -= 10
        tail, head = merge_back(fac_ref, base, vector(val_ref, place), vector(val_ref, place + 5), first, last)
        latter = (row % (2 * distance)) >= distance
        first = [jnp.where(latter, turn(head[a], distance), first[a]) for a in N]
        last = [jnp.where(latter, turn(last[a], distance), tail[a]) for a in N]
    d1 = diagonal(step_ref, 1)
    d2 = diagonal(step_ref, 2)
    part = mv(block(fac_ref, 25), first)
    x1 = vplus(vplus(vector(val_ref, 0), [d2 * value for value in part]), mv(block(fac_ref, 50), last))
    far = mv(block(fac_ref, 75), last)
    near = mv(shifted(half_jacobian(jac_ref, 1), e), part)
    x2 = vplus(vector(val_ref, 5), vminus(near, [d1 * value for value in far]))
    for a in N:
        out_ref[a, pl.ds(0, CHUNKS, stride=CELLS), :] = first[a]
        out_ref[a, pl.ds(1, CHUNKS, stride=CELLS), :] = x1[a]
        out_ref[a, pl.ds(2, CHUNKS, stride=CELLS), :] = x2[a]
        out_ref[a, pl.ds(3, CHUNKS, stride=CELLS), :] = last[a]


INTERPRET = False


VMEM = pl.BlockSpec(memory_space=pltpu.VMEM)
HBM = pl.BlockSpec(memory_space=pltpu.MemorySpace.HBM)


def kept(shape, dtype=jnp.float32):
    return jax.ShapeDtypeStruct(shape, dtype) if INTERPRET else pltpu.VMEM(shape, dtype)


def inside(values):
    return values if INTERPRET else [pltpu.with_memory_space_constraint(value, pltpu.VMEM) for value in values]


def outside(values):
    return values if INTERPRET else [pltpu.with_memory_space_constraint(value, pltpu.MemorySpace.HBM) for value in values]


def run(kernel, name, outs, args, scratch, far_args=0, far_outs=0):
    return pl.pallas_call(
        kernel,
        out_shape=outs,
        in_specs=[HBM] * far_args + [VMEM] * (len(args) - far_args),
        out_specs=[HBM] * far_outs + [VMEM] * (len(outs) - far_outs),
        scratch_shapes=scratch,
        compiler_params=pltpu.CompilerParams(vmem_limit_bytes=12 << 20),
        interpret=INTERPRET,
        name=name,
    )(*outside(args[:far_args]), *inside(args[far_args:]))


def tiles(count):
    return pltpu.VMEM((8 * count, LANES), jnp.float32)


def shards(jacobian, time_step, source, cross_flux):
    count = lax.axis_size("cross")
    cells = CHUNKS * CELLS
    before = lax.ppermute(cross_flux, "cross", [(i, i + 1) for i in range(count - 1)])
    after = lax.ppermute(cross_flux, "cross", [(i + 1, i) for i in range(count - 1)])
    jac, step, src, flux, factors, part = run(
        factor_kernel,
        "factor",
        [
            kept((5, 5, cells, LANES)),
            kept((cells, LANES)),
            kept((5, cells, LANES), jnp.bfloat16),
            kept((5, cells, LANES), jnp.bfloat16),
            kept((8 * TILES, LANES)),
            kept((120, LANES)),
        ],
        [jacobian, time_step, source, cross_flux],
        [tiles(120), pltpu.SemaphoreType.DMA((8,))],
        far_args=4,
    )
    packet, values = run(
        rhs_kernel,
        "right_side",
        [kept((SENT, LANES)), kept((8 * VALUES, LANES))],
        [jac, step, src, flux, before, after, factors, part],
        [pltpu.VMEM((5, cells, LANES), jnp.float32), tiles(16)],
    )
    packets = lax.all_gather(packet, "line", axis=0)
    return run(
        solve_kernel,
        "solve",
        [jax.ShapeDtypeStruct((5, cells, LANES), jnp.float32)],
        [packets, jac, step, factors, values],
        [
            pltpu.VMEM((5, cells, LANES), jnp.float32),
            tiles(2 * ROWS),
            tiles(4 * STAGE),
            tiles(16),
            tiles(5),
            pltpu.SemaphoreType.DMA((5,)),
        ],
        far_outs=1,
    )[0]


def solution(mesh):
    placed = (
        P(None, None, "line", "cross"),
        P("line", "cross"),
        P(None, "line", "cross"),
        P(None, "line", "cross"),
    )
    return jax.shard_map(
        shards, mesh=mesh, in_specs=placed, out_specs=P(None, "line", "cross"), check_vma=False
    )
```

```python
import jax
import jax.numpy as jnp
from jax import lax
from jax.experimental import pallas as pl
from jax.experimental.pallas import tpu as pltpu
from jax.sharding import PartitionSpec as P

NZ = 8
damping = 0.05

CHUNKS = 8
CELLS = 4
LANES = 128
SENT = 125
ROWS = 128
INV, LOW, UPP, VLOW, VUPP = (25 * k for k in range(5))
STAGE = 125
N = range(5)


def tile(ref, number):
    return ref[8 * number : 8 * number + 8, :]


def block(ref, base):
    return [[tile(ref, base + 5 * a + b) for b in N] for a in N]


def vector(ref, base):
    return [tile(ref, base + a) for a in N]


def keep(ref, base, matrix):
    for a in N:
        for b in N:
            ref[8 * (base + 5 * a + b) : 8 * (base + 5 * a + b) + 8, :] = matrix[a][b]


def keep_vector(ref, base, values):
    for a in N:
        ref[8 * (base + a) : 8 * (base + a) + 8, :] = values[a]


def total(terms):
    result = terms[0]
    for term in terms[1:]:
        result = result + term
    return result


def mm(left, right):
    return [[total([left[a][k] * right[k][b] for k in N]) for b in N] for a in N]


def mv(left, right):
    return [total([left[a][k] * right[k] for k in N]) for a in N]


def plus(left, right):
    return [[left[a][b] + right[a][b] for b in N] for a in N]


def minus(left, right):
    return [[left[a][b] - right[a][b] for b in N] for a in N]


def negative(matrix):
    return [[-matrix[a][b] for b in N] for a in N]


def vplus(left, right):
    return [left[a] + right[a] for a in N]


def vminus(left, right):
    return [left[a] - right[a] for a in N]


def scaled(factor, matrix):
    return [[factor * matrix[a][b] for b in N] for a in N]


def shifted(matrix, amount):
    return [[matrix[a][b] + amount if a == b else matrix[a][b] for b in N] for a in N]


def turn(value, count):
    return pltpu.roll(value, count % CHUNKS, axis=0)


def flipped(matrix):
    return [[matrix[b][a] for b in N] for a in N]


def mturn(matrix, count):
    return [[turn(matrix[a][b], count) for b in N] for a in N]


def vturn(values, count):
    return [turn(values[a], count) for a in N]


def inverse(matrix):
    m = [list(row) for row in matrix]
    for k in N:
        pivot = 1.0 / m[k][k]
        for b in N:
            m[k][b] = pivot if b == k else m[k][b] * pivot
        for a in N:
            if a != k:
                factor = m[a][k]
                for b in N:
                    m[a][b] = -factor * pivot if b == k else m[a][b] - factor * m[k][b]
    return m


def inverse_and_solved(matrix, *sides):
    m = [list(row) + [side[a][b] for side in sides for b in N] for a, row in enumerate(matrix)]
    width = len(m[0])
    for k in N:
        pivot = 1.0 / m[k][k]
        for b in range(width):
            m[k][b] = pivot if b == k else m[k][b] * pivot
        for a in N:
            if a != k:
                factor = m[a][k]
                for b in range(width):
                    m[a][b] = -factor * pivot if b == k else m[a][b] - factor * m[k][b]
    return [[row[at : at + 5] for row in m] for at in range(0, width, 5)]


def half_jacobian(jac_ref, cell):
    half = [[None] * 5 for _ in N]
    for a in N:
        for b in range(a, 5):
            half[a][b] = half[b][a] = 0.5 * jac_ref[a, b, pl.ds(cell, CHUNKS, stride=CELLS), :]
    return half


def half_before(half_last):
    first = lax.broadcasted_iota(jnp.int32, (CHUNKS, LANES), 0) == 0
    result = [[None] * 5 for _ in N]
    for a in N:
        for b in range(a, 5):
            outside = 1.0 - damping if a == b else 0.0
            result[a][b] = result[b][a] = jnp.where(first, outside, turn(half_last[a][b], 1))
    return result


def diagonal(step_ref, cell):
    return 1.0 / step_ref[pl.ds(cell, CHUNKS, stride=CELLS), :] + 2.0 * damping


def stage(fac_ref, base, low, own, nxt, upp, distance):
    inv, vlow, vupp = inverse_and_solved(plus(own, nxt), low, upp)
    keep(fac_ref, base + INV, inv)
    keep(fac_ref, base + LOW, low)
    keep(fac_ref, base + UPP, upp)
    keep(fac_ref, base + VLOW, vlow)
    keep(fac_ref, base + VUPP, vupp)
    own = minus(own, mm(low, mturn(vupp, distance)))
    nxt = minus(nxt, mm(upp, mturn(vlow, -distance)))
    low = negative(mm(low, mturn(vlow, distance)))
    upp = negative(mm(upp, mturn(vupp, -distance)))
    return low, own, nxt, upp


def stage_rhs(fac_ref, base, own, nxt, distance):
    value = mv(block(fac_ref, base + INV), vplus(own, nxt))
    own = vminus(own, mv(block(fac_ref, base + LOW), vturn(value, distance)))
    nxt = vminus(nxt, mv(block(fac_ref, base + UPP), vturn(value, -distance)))
    return value, own, nxt


def stage_back(fac_ref, base, value, before, after):
    return vminus(
        vminus(value, mv(block(fac_ref, base + VLOW), before)), mv(block(fac_ref, base + VUPP), after)
    )


def merge(fac_ref, base, former, latter, upp, low):
    head_head, head_tail, tail_head, tail_tail = former
    inv_head, carry, reach = inverse_and_solved(latter[0], low, latter[1])
    inv_tail, tail_by_head, tail_by_tail = inverse_and_solved(
        plus(tail_tail, mm(upp, carry)), tail_head, mm(upp, reach)
    )
    head_by_head = mm(carry, tail_by_head)
    head_by_tail = minus(reach, mm(carry, tail_by_tail))
    for number, kept in enumerate(
        (
            inv_head,
            carry,
            inv_tail,
            upp,
            head_tail,
            latter[2],
            tail_by_head,
            tail_by_tail,
            head_by_head,
            head_by_tail,
        )
    ):
        keep(fac_ref, base + 25 * number, kept)
    return (
        minus(head_head, mm(head_tail, tail_by_head)),
        mm(head_tail, tail_by_tail),
        negative(mm(latter[2], head_by_head)),
        minus(latter[3], mm(latter[2], head_by_tail)),
    )


def merge_rhs(fac_ref, base, former, latter):
    head = mv(block(fac_ref, base), latter[0])
    tail = mv(block(fac_ref, base + 50), vminus(former[1], mv(block(fac_ref, base + 75), head)))
    head = vplus(head, mv(block(fac_ref, base + 25), tail))
    return (
        tail,
        head,
        vminus(former[0], mv(block(fac_ref, base + 100), tail)),
        vminus(latter[1], mv(block(fac_ref, base + 125), head)),
    )


def merge_back(fac_ref, base, tail, head, first, last):
    tail = vplus(
        vminus(tail, mv(block(fac_ref, base + 150), first)), mv(block(fac_ref, base + 175), last)
    )
    head = vminus(
        vminus(head, mv(block(fac_ref, base + 200), first)), mv(block(fac_ref, base + 225), last)
    )
    return tail, head


def rows_of_last(ref, group):
    return ref[pl.ds(64 * group + CHUNKS - WIDTH, 8, stride=8), :]


WIDTH = 2
MERGES = tuple((1 << k, 100 + 250 * k) for k in range(WIDTH.bit_length() - 1))
CLOSE = 100 + 250 * len(MERGES)
STAGES = tuple((WIDTH << k, CLOSE + 100 + 125 * k) for k in range((CHUNKS // WIDTH).bit_length() - 1))
TILES = CLOSE + 100 + 125 * len(STAGES)
VALUES = 15 + 10 * len(MERGES) + 5 * len(STAGES)


def factor_kernel(
    jac_hbm, step_hbm, src_hbm, flux_hbm, jac_ref, step_ref, src_ref, flux_ref, fac_ref, pack_ref, end_ref, sems
):
    needed = [pltpu.make_async_copy(jac_hbm.at[a, a:], jac_ref.at[a, a:], sems.at[a]) for a in N]
    needed.append(pltpu.make_async_copy(step_hbm, step_ref, sems.at[5]))
    later = [
        pltpu.make_async_copy(src_hbm, src_ref, sems.at[6]),
        pltpu.make_async_copy(flux_hbm, flux_ref, sems.at[7]),
    ]
    for copy in needed + later:
        copy.start()
    for copy in needed:
        copy.wait()
    factor(jac_ref, step_ref, fac_ref, pack_ref, end_ref)
    for copy in later:
        copy.wait()


def factor(jac_ref, step_ref, fac_ref, pack_ref, end_ref):
    e = damping
    h0 = half_jacobian(jac_ref, 0)
    h1 = half_jacobian(jac_ref, 1)
    h2 = half_jacobian(jac_ref, 2)
    h3 = half_jacobian(jac_ref, 3)
    d1 = diagonal(step_ref, 1)
    d2 = diagonal(step_ref, 2)
    h0p, h1p, h2p, h3p = shifted(h0, e), shifted(h1, e), shifted(h2, e), shifted(h3, e)
    h0m, h1m, h2m, h3m = shifted(h0, -e), shifted(h1, -e), shifted(h2, -e), shifted(h3, -e)
    inv, by_low, by_upp = inverse_and_solved(shifted(mm(h2m, h1p), d1 * d2), h0p, mm(h2m, h3m))
    by_end = mm(flipped(inv), h3m)
    pair = mm(h2p, h1p)
    group = (
        shifted(mm(h1m, scaled(d2, by_low)), diagonal(step_ref, 0)),
        mm(h1m, by_upp),
        negative(mm(pair, by_low)),
        shifted(mm(scaled(d1, h2p), by_end), diagonal(step_ref, 3)),
    )
    keep(fac_ref, 0, inv)
    keep(fac_ref, 25, by_low)
    keep(fac_ref, 50, by_upp)
    keep(fac_ref, 75, by_end)
    for distance, base in MERGES:
        latter = tuple(mturn(part, -distance) for part in group)
        group = merge(fac_ref, base, group, latter, mturn(h0m, -distance), mturn(h3p, 1 - distance))
    head_head, head_tail, tail_head, tail_tail = group
    inv, reach = inverse_and_solved(head_head, head_tail)
    through = mm(tail_head, inv)
    into = mm(h0m, inv)
    keep(fac_ref, CLOSE, inv)
    keep(fac_ref, CLOSE + 25, reach)
    keep(fac_ref, CLOSE + 50, through)
    keep(fac_ref, CLOSE + 75, into)
    own = minus(tail_tail, mm(tail_head, reach))
    upp = mturn(negative(mm(h0m, reach)), -WIDTH)
    low, nxt = through, into
    if STAGES:
        link = shifted(half_before(h3), e)
        low, nxt = mm(through, link), mm(into, link)
    nxt = mturn(nxt, -WIDTH)
    for distance, base in STAGES:
        low, own, nxt, upp = stage(fac_ref, base, low, own, nxt, upp, distance)
    keep(end_ref, 0, low)
    keep(end_ref, 25, own)
    keep(end_ref, 50, nxt)
    keep(end_ref, 75, upp)
    place = 100
    for a in N:
        for b in range(a, 5):
            end_ref[8 * place : 8 * place + 8, :] = turn(h3p[a][b], 1 - WIDTH)
            place += 1
    for number in range(15):
        pack_ref[8 * number : 8 * number + 8, :] = rows_of_last(end_ref, number)


def rhs_kernel(
    jac_ref, step_ref, src_ref, flux_ref, even_ref, odd_ref, fac_ref, part_ref, pack_ref, val_ref, res_ref, end_ref
):
    e = damping
    lane = lax.broadcasted_iota(jnp.int32, (CHUNKS * CELLS, LANES), 1)
    is_even = lax.axis_index("cross") % 2 == 0
    for a in N:
        flux = flux_ref[a].astype(jnp.float32)
        even_swap = even_ref[a].astype(jnp.float32)
        odd_swap = odd_ref[a].astype(jnp.float32)
        after = jnp.where(is_even, even_swap, odd_swap)
        before = jnp.where(is_even, odd_swap, even_swap)
        upper = pltpu.roll(jnp.where(lane < NZ, after, flux), LANES - NZ, axis=1)
        lower = pltpu.roll(jnp.where(lane >= LANES - NZ, before, flux), NZ, axis=1)
        res_ref[a] = src_ref[a].astype(jnp.float32) - 0.5 * (upper - lower)
    r0, r1, r2, r3 = ([res_ref[a, pl.ds(cell, CHUNKS, stride=CELLS), :] for a in N] for cell in range(CELLS))
    h1 = half_jacobian(jac_ref, 1)
    h2 = half_jacobian(jac_ref, 2)
    d1 = diagonal(step_ref, 1)
    d2 = diagonal(step_ref, 2)
    inv = block(fac_ref, 0)
    part = mv(inv, r1)
    x1 = vminus([d2 * value for value in part], mv(inv, mv(shifted(h2, -e), r2)))
    x2 = vplus(mv(shifted(h1, e), part), [d1 * value for value in mv(flipped(inv), r2)])
    keep_vector(val_ref, 0, x1)
    keep_vector(val_ref, 5, x2)
    head = vminus(r0, mv(shifted(h1, -e), x1))
    tail = vplus(r3, mv(shifted(h2, e), x2))
    place = 10
    for distance, base in MERGES:
        latter = (vturn(head, -distance), vturn(tail, -distance))
        inner_tail, inner_head, head, tail = merge_rhs(fac_ref, base, (head, tail), latter)
        keep_vector(val_ref, place, inner_tail)
        keep_vector(val_ref, place + 5, inner_head)
        place += 10
    keep_vector(val_ref, place, mv(block(fac_ref, CLOSE), head))
    own = vminus(tail, mv(block(fac_ref, CLOSE + 50), head))
    nxt = vturn([-value for value in mv(block(fac_ref, CLOSE + 75), head)], -WIDTH)
    for distance, base in STAGES:
        place += 5
        value, own, nxt = stage_rhs(fac_ref, base, own, nxt, distance)
        keep_vector(val_ref, place, value)
    end_ref[...] = jnp.zeros_like(end_ref)
    keep_vector(end_ref, 3, own)
    keep_vector(end_ref, 8, nxt)
    pack_ref[:112, :] = part_ref[:112, :]
    row = lax.broadcasted_iota(jnp.int32, (8, LANES), 0)
    pack_ref[112:120, :] = jnp.where(row < 3, part_ref[112:120, :], rows_of_last(end_ref, 0))
    pack_ref[120:125, :] = rows_of_last(end_ref, 1)[:5]


def solve_kernel(sent_ref, jac_ref, step_ref, fac_ref, val_ref, out_hbm, out_ref, all_ref, red_ref, x_ref, w_ref, sems):
    solve(sent_ref, jac_ref, step_ref, fac_ref, val_ref, out_ref, all_ref, red_ref, x_ref, w_ref)
    copies = [pltpu.make_async_copy(out_ref.at[a], out_hbm.at[a], sems.at[a]) for a in N]
    for copy in copies:
        copy.start()
    for copy in copies:
        copy.wait()


def solve(sent_ref, jac_ref, step_ref, fac_ref, val_ref, out_ref, all_ref, red_ref, x_ref, w_ref):
    e = damping
    for device in range(16):
        all_ref[ROWS * device : ROWS * device + SENT, :] = sent_ref[device]
    row = lax.broadcasted_iota(jnp.int32, (CHUNKS, LANES), 0)

    def packed(parity, number):
        return all_ref[pl.ds(parity * ROWS + number, 8, stride=2 * ROWS), :]

    def packed_block(parity, base):
        return [[packed(parity, base + 5 * a + b) for b in N] for a in N]

    def packed_vector(parity, base):
        return [packed(parity, base + a) for a in N]

    def packed_symmetric(parity, base):
        result = [[None] * 5 for _ in N]
        for a in N:
            for b in range(a, 5):
                result[a][b] = result[b][a] = packed(parity, base)
                base += 1
        return result

    m_even = packed_symmetric(0, 100)
    m_odd = packed_symmetric(1, 100)
    inv, vlow, vupp = inverse_and_solved(
        plus(packed_block(0, 25), mm(packed_block(1, 50), m_even)), packed_block(0, 0), packed_block(1, 75)
    )
    value = mv(inv, vplus(packed_vector(0, 115), packed_vector(1, 120)))
    keep(red_ref, VLOW, vlow)
    keep(red_ref, VUPP, vupp)
    keep_vector(x_ref, 4, value)
    cross = mm(packed_block(1, 0), m_even)
    own = minus(packed_block(1, 25), mm(cross, vupp))
    low = negative(mm(cross, vlow))
    own_rhs = vminus(packed_vector(1, 115), mv(cross, value))
    back = packed_block(0, 75)
    nxt = minus(packed_block(0, 50), mm(back, vlow))
    upp = negative(mm(back, vupp))
    nxt_rhs = vminus(packed_vector(0, 120), mv(back, value))
    first, last = row == 0, row == CHUNKS - 1
    low = mm(low, mturn(m_odd, 1))
    low = [[jnp.where(first, 0.0, low[a][b]) for b in N] for a in N]
    nxt = mm(mturn(nxt, -1), m_odd)
    nxt = [[jnp.where(last, 0.0, nxt[a][b]) for b in N] for a in N]
    upp = [[jnp.where(last, 0.0, turn(upp[a][b], -1)) for b in N] for a in N]
    nxt_rhs = [jnp.where(last, 0.0, turn(nxt_rhs[a], -1)) for a in N]
    levels = ((1, 1), (2, 2), (3, 4))
    values = []
    for number, distance in levels:
        low, own, nxt, upp = stage(red_ref, number * STAGE, low, own, nxt, upp, distance)
        value, own_rhs, nxt_rhs = stage_rhs(red_ref, number * STAGE, own_rhs, nxt_rhs, distance)
        values.append(value)
    x = mv(inverse(plus(own, nxt)), vplus(own_rhs, nxt_rhs))
    for number, distance in reversed(levels):
        found = stage_back(red_ref, number * STAGE, values[number - 1], vturn(x, distance), vturn(x, -distance))
        chosen = (row % (2 * distance)) == distance - 1
        x = [jnp.where(chosen, found[a], x[a]) for a in N]
    w_odd = mv(m_odd, x)
    before = [jnp.where(first, 0.0, turn(w_odd[a], 1)) for a in N]
    x_even = stage_back(red_ref, 0, vector(x_ref, 4), before, x)
    w_even = mv(m_even, x_even)
    position = lax.axis_index("line")
    half, odd = position // 2, position % 2
    is_odd = odd == 1
    for a in N:
        w_ref[8 * a : 8 * a + 8, :] = jnp.where(is_odd, w_even[a], before[a])
        x_ref[8 * a : 8 * a + 8, :] = jnp.where(is_odd, x[a], x_even[a])
    ends = [jnp.broadcast_to(x_ref[pl.ds(8 * a + half, 1), :], (CHUNKS, LANES)) for a in N]
    w = [jnp.broadcast_to(w_ref[pl.ds(8 * a + half, 1), :], (CHUNKS, LANES)) for a in N]

    def neighbour(values, distance):
        return [jnp.where(row < distance, w[a], turn(values[a], distance)) for a in N]

    last = ends
    place = VALUES - 5
    for distance, base in reversed(STAGES):
        found = stage_back(fac_ref, base, vector(val_ref, place), neighbour(last, distance), vturn(last, -distance))
        place -= 5
        chosen = (row % (2 * distance)) == distance - WIDTH
        last = [jnp.where(chosen, found[a], last[a]) for a in N]
    if STAGES:
        w = mv(shifted(half_before(half_jacobian(jac_ref, 3)), e), neighbour(last, WIDTH))
    first = vplus(
        vector(val_ref, place), vminus(mv(block(fac_ref, CLOSE), w), mv(block(fac_ref, CLOSE + 25), last))
    )
    for distance, base in reversed(MERGES):
        place -= 10
        tail, head = merge_back(fac_ref, base, vector(val_ref, place), vector(val_ref, place + 5), first, last)
        latter = (row % (2 * distance)) >= distance
        first = [jnp.where(latter, turn(head[a], distance), first[a]) for a in N]
        last = [jnp.where(latter, turn(last[a], distance), tail[a]) for a in N]
    d1 = diagonal(step_ref, 1)
    d2 = diagonal(step_ref, 2)
    part = mv(block(fac_ref, 25), first)
    x1 = vplus(vplus(vector(val_ref, 0), [d2 * value for value in part]), mv(block(fac_ref, 50), last))
    far = mv(block(fac_ref, 75), last)
    near = mv(shifted(half_jacobian(jac_ref, 1), e), part)
    x2 = vplus(vector(val_ref, 5), vminus(near, [d1 * value for value in far]))
    for a in N:
        out_ref[a, pl.ds(0, CHUNKS, stride=CELLS), :] = first[a]
        out_ref[a, pl.ds(1, CHUNKS, stride=CELLS), :] = x1[a]
        out_ref[a, pl.ds(2, CHUNKS, stride=CELLS), :] = x2[a]
        out_ref[a, pl.ds(3, CHUNKS, stride=CELLS), :] = last[a]


INTERPRET = False


VMEM = pl.BlockSpec(memory_space=pltpu.VMEM)
HBM = pl.BlockSpec(memory_space=pltpu.MemorySpace.HBM)


def kept(shape, dtype=jnp.float32):
    return jax.ShapeDtypeStruct(shape, dtype) if INTERPRET else pltpu.VMEM(shape, dtype)


def inside(values):
    return values if INTERPRET else [pltpu.with_memory_space_constraint(value, pltpu.VMEM) for value in values]


def outside(values):
    return values if INTERPRET else [pltpu.with_memory_space_constraint(value, pltpu.MemorySpace.HBM) for value in values]


def run(kernel, name, outs, args, scratch, far_args=0, far_outs=0):
    return pl.pallas_call(
        kernel,
        out_shape=outs,
        in_specs=[HBM] * far_args + [VMEM] * (len(args) - far_args),
        out_specs=[HBM] * far_outs + [VMEM] * (len(outs) - far_outs),
        scratch_shapes=scratch,
        compiler_params=pltpu.CompilerParams(vmem_limit_bytes=12 << 20),
        interpret=INTERPRET,
        name=name,
    )(*outside(args[:far_args]), *inside(args[far_args:]))


def tiles(count):
    return pltpu.VMEM((8 * count, LANES), jnp.float32)


def shards(jacobian, time_step, source, cross_flux):
    count = lax.axis_size("cross")
    cells = CHUNKS * CELLS
    even_swap, odd_swap = (
        lax.ppermute(
            cross_flux,
            "cross",
            [pair for i in range(start, count - 1, 2) for pair in ((i, i + 1), (i + 1, i))],
        )
        for start in (0, 1)
    )
    jac, step, src, flux, factors, part = run(
        factor_kernel,
        "factor",
        [
            kept((5, 5, cells, LANES)),
            kept((cells, LANES)),
            kept((5, cells, LANES), jnp.bfloat16),
            kept((5, cells, LANES), jnp.bfloat16),
            kept((8 * TILES, LANES)),
            kept((120, LANES)),
        ],
        [jacobian, time_step, source, cross_flux],
        [tiles(120), pltpu.SemaphoreType.DMA((8,))],
        far_args=4,
    )
    packet, values = run(
        rhs_kernel,
        "right_side",
        [kept((SENT, LANES)), kept((8 * VALUES, LANES))],
        [jac, step, src, flux, even_swap, odd_swap, factors, part],
        [pltpu.VMEM((5, cells, LANES), jnp.float32), tiles(16)],
    )
    packets = lax.all_gather(packet, "line", axis=0)
    return run(
        solve_kernel,
        "solve",
        [jax.ShapeDtypeStruct((5, cells, LANES), jnp.float32)],
        [packets, jac, step, factors, values],
        [
            pltpu.VMEM((5, cells, LANES), jnp.float32),
            tiles(2 * ROWS),
            tiles(4 * STAGE),
            tiles(16),
            tiles(5),
            pltpu.SemaphoreType.DMA((5,)),
        ],
        far_outs=1,
    )[0]


def solution(mesh):
    placed = (
        P(None, None, "line", "cross"),
        P("line", "cross"),
        P(None, "line", "cross"),
        P(None, "line", "cross"),
    )
    return jax.shard_map(
        shards, mesh=mesh, in_specs=placed, out_specs=P(None, "line", "cross"), check_vma=False
    )
```

```python
import jax
import jax.numpy as jnp
from jax import lax
from jax.experimental import pallas as pl
from jax.experimental.pallas import tpu as pltpu
from jax.sharding import PartitionSpec as P

NZ = 8
damping = 0.05

CHUNKS = 8
CELLS = 4
LANES = 128
SENT = 125
ROWS = 128
INV, LOW, UPP, VLOW, VUPP = (25 * k for k in range(5))
STAGE = 125
N = range(5)


def tile(ref, number):
    return ref[8 * number : 8 * number + 8, :]


def block(ref, base):
    return [[tile(ref, base + 5 * a + b) for b in N] for a in N]


def vector(ref, base):
    return [tile(ref, base + a) for a in N]


def keep(ref, base, matrix):
    for a in N:
        for b in N:
            ref[8 * (base + 5 * a + b) : 8 * (base + 5 * a + b) + 8, :] = matrix[a][b]


def keep_vector(ref, base, values):
    for a in N:
        ref[8 * (base + a) : 8 * (base + a) + 8, :] = values[a]


def total(terms):
    result = terms[0]
    for term in terms[1:]:
        result = result + term
    return result


def mm(left, right):
    return [[total([left[a][k] * right[k][b] for k in N]) for b in N] for a in N]


def mv(left, right):
    return [total([left[a][k] * right[k] for k in N]) for a in N]


def plus(left, right):
    return [[left[a][b] + right[a][b] for b in N] for a in N]


def minus(left, right):
    return [[left[a][b] - right[a][b] for b in N] for a in N]


def negative(matrix):
    return [[-matrix[a][b] for b in N] for a in N]


def vplus(left, right):
    return [left[a] + right[a] for a in N]


def vminus(left, right):
    return [left[a] - right[a] for a in N]


def scaled(factor, matrix):
    return [[factor * matrix[a][b] for b in N] for a in N]


def shifted(matrix, amount):
    return [[matrix[a][b] + amount if a == b else matrix[a][b] for b in N] for a in N]


def turn(value, count):
    return pltpu.roll(value, count % CHUNKS, axis=0)


def flipped(matrix):
    return [[matrix[b][a] for b in N] for a in N]


def mturn(matrix, count):
    return [[turn(matrix[a][b], count) for b in N] for a in N]


def vturn(values, count):
    return [turn(values[a], count) for a in N]


def inverse_and_solved(matrix, *sides):
    m = [list(row) + [side[a][b] for side in sides for b in N] for a, row in enumerate(matrix)]
    width = len(m[0])
    for k in N:
        pivot = 1.0 / m[k][k]
        for b in range(width):
            m[k][b] = pivot if b == k else m[k][b] * pivot
        for a in N:
            if a != k:
                factor = m[a][k]
                for b in range(width):
                    m[a][b] = -factor * pivot if b == k else m[a][b] - factor * m[k][b]
    return [[row[at : at + 5] for row in m] for at in range(0, width, 5)]


def solved(matrix, values, *sides):
    m = [list(row) + [values[a]] + [side[a][b] for side in sides for b in N] for a, row in enumerate(matrix)]
    width = len(m[0])
    for k in N:
        pivot = 1.0 / m[k][k]
        for b in range(k + 1, width):
            m[k][b] = m[k][b] * pivot
        for a in N:
            if a != k:
                for b in range(k + 1, width):
                    m[a][b] = m[a][b] - m[a][k] * m[k][b]
    return [row[5] for row in m], [[row[at : at + 5] for row in m] for at in range(6, width, 5)]


def half_jacobian(jac_ref, cell):
    half = [[None] * 5 for _ in N]
    for a in N:
        for b in range(a, 5):
            half[a][b] = half[b][a] = 0.5 * jac_ref[a, b, pl.ds(cell, CHUNKS, stride=CELLS), :]
    return half


def half_before(half_last):
    first = lax.broadcasted_iota(jnp.int32, (CHUNKS, LANES), 0) == 0
    result = [[None] * 5 for _ in N]
    for a in N:
        for b in range(a, 5):
            outside = 1.0 - damping if a == b else 0.0
            result[a][b] = result[b][a] = jnp.where(first, outside, turn(half_last[a][b], 1))
    return result


def diagonal(step_ref, cell):
    return 1.0 / step_ref[pl.ds(cell, CHUNKS, stride=CELLS), :] + 2.0 * damping


def next_rows(low, own, nxt, upp, vlow, vupp, distance):
    vlow_before, vupp_before = mturn(vlow, distance), mturn(vupp, distance)
    vlow_after, vupp_after = vlow_before, vupp_before
    if 2 * distance != CHUNKS:
        vlow_after, vupp_after = mturn(vlow, -distance), mturn(vupp, -distance)
    return (
        negative(mm(low, vlow_before)),
        minus(own, mm(low, vupp_before)),
        minus(nxt, mm(upp, vlow_after)),
        negative(mm(upp, vupp_after)),
    )


def stage(fac_ref, base, low, own, nxt, upp, distance):
    inv, vlow, vupp = inverse_and_solved(plus(own, nxt), low, upp)
    keep(fac_ref, base + INV, inv)
    keep(fac_ref, base + LOW, low)
    keep(fac_ref, base + UPP, upp)
    keep(fac_ref, base + VLOW, vlow)
    keep(fac_ref, base + VUPP, vupp)
    return next_rows(low, own, nxt, upp, vlow, vupp, distance)


def stage_rhs(fac_ref, base, own, nxt, distance):
    value = mv(block(fac_ref, base + INV), vplus(own, nxt))
    own = vminus(own, mv(block(fac_ref, base + LOW), vturn(value, distance)))
    nxt = vminus(nxt, mv(block(fac_ref, base + UPP), vturn(value, -distance)))
    return value, own, nxt


def stage_back(fac_ref, base, value, before, after):
    return vminus(
        vminus(value, mv(block(fac_ref, base + VLOW), before)), mv(block(fac_ref, base + VUPP), after)
    )


def merge(fac_ref, base, former, latter, upp, low):
    head_head, head_tail, tail_head, tail_tail = former
    inv_head, carry, reach = inverse_and_solved(latter[0], low, latter[1])
    inv_tail, tail_by_head, tail_by_tail = inverse_and_solved(
        plus(tail_tail, mm(upp, carry)), tail_head, mm(upp, reach)
    )
    head_by_head = mm(carry, tail_by_head)
    head_by_tail = minus(reach, mm(carry, tail_by_tail))
    for number, kept in enumerate(
        (
            inv_head,
            carry,
            inv_tail,
            upp,
            head_tail,
            latter[2],
            tail_by_head,
            tail_by_tail,
            head_by_head,
            head_by_tail,
        )
    ):
        keep(fac_ref, base + 25 * number, kept)
    return (
        minus(head_head, mm(head_tail, tail_by_head)),
        mm(head_tail, tail_by_tail),
        negative(mm(latter[2], head_by_head)),
        minus(latter[3], mm(latter[2], head_by_tail)),
    )


def merge_rhs(fac_ref, base, former, latter):
    head = mv(block(fac_ref, base), latter[0])
    tail = mv(block(fac_ref, base + 50), vminus(former[1], mv(block(fac_ref, base + 75), head)))
    head = vplus(head, mv(block(fac_ref, base + 25), tail))
    return (
        tail,
        head,
        vminus(former[0], mv(block(fac_ref, base + 100), tail)),
        vminus(latter[1], mv(block(fac_ref, base + 125), head)),
    )


def merge_back(fac_ref, base, tail, head, first, last):
    tail = vplus(
        vminus(tail, mv(block(fac_ref, base + 150), first)), mv(block(fac_ref, base + 175), last)
    )
    head = vminus(
        vminus(head, mv(block(fac_ref, base + 200), first)), mv(block(fac_ref, base + 225), last)
    )
    return tail, head


def rows_of_last(ref, group):
    return ref[pl.ds(64 * group + CHUNKS - WIDTH, 8, stride=8), :]


WIDTH = 2
MERGES = tuple((1 << k, 100 + 250 * k) for k in range(WIDTH.bit_length() - 1))
CLOSE = 100 + 250 * len(MERGES)
STAGES = tuple((WIDTH << k, CLOSE + 100 + 125 * k) for k in range((CHUNKS // WIDTH).bit_length() - 1))
TILES = CLOSE + 100 + 125 * len(STAGES)
VALUES = 15 + 10 * len(MERGES) + 5 * len(STAGES)


def factor_kernel(
    jac_hbm, step_hbm, src_hbm, flux_hbm, jac_ref, step_ref, src_ref, flux_ref, fac_ref, pack_ref, end_ref, sems
):
    needed = [pltpu.make_async_copy(jac_hbm.at[a, a:], jac_ref.at[a, a:], sems.at[a]) for a in N]
    needed.append(pltpu.make_async_copy(step_hbm, step_ref, sems.at[5]))
    later = [
        pltpu.make_async_copy(src_hbm, src_ref, sems.at[6]),
        pltpu.make_async_copy(flux_hbm, flux_ref, sems.at[7]),
    ]
    for copy in needed + later:
        copy.start()
    for copy in needed:
        copy.wait()
    factor(jac_ref, step_ref, fac_ref, pack_ref, end_ref)
    for copy in later:
        copy.wait()


def factor(jac_ref, step_ref, fac_ref, pack_ref, end_ref):
    e = damping
    h0 = half_jacobian(jac_ref, 0)
    h1 = half_jacobian(jac_ref, 1)
    h2 = half_jacobian(jac_ref, 2)
    h3 = half_jacobian(jac_ref, 3)
    d1 = diagonal(step_ref, 1)
    d2 = diagonal(step_ref, 2)
    h0p, h1p, h2p, h3p = shifted(h0, e), shifted(h1, e), shifted(h2, e), shifted(h3, e)
    h0m, h1m, h2m, h3m = shifted(h0, -e), shifted(h1, -e), shifted(h2, -e), shifted(h3, -e)
    inv, by_low, by_upp = inverse_and_solved(shifted(mm(h2m, h1p), d1 * d2), h0p, mm(h2m, h3m))
    by_end = mm(flipped(inv), h3m)
    pair = mm(h2p, h1p)
    group = (
        shifted(mm(h1m, scaled(d2, by_low)), diagonal(step_ref, 0)),
        mm(h1m, by_upp),
        negative(mm(pair, by_low)),
        shifted(mm(scaled(d1, h2p), by_end), diagonal(step_ref, 3)),
    )
    keep(fac_ref, 0, inv)
    keep(fac_ref, 25, by_low)
    keep(fac_ref, 50, by_upp)
    keep(fac_ref, 75, by_end)
    for distance, base in MERGES:
        latter = tuple(mturn(part, -distance) for part in group)
        group = merge(fac_ref, base, group, latter, mturn(h0m, -distance), mturn(h3p, 1 - distance))
    head_head, head_tail, tail_head, tail_tail = group
    inv, reach = inverse_and_solved(head_head, head_tail)
    through = mm(tail_head, inv)
    into = mm(h0m, inv)
    keep(fac_ref, CLOSE, inv)
    keep(fac_ref, CLOSE + 25, reach)
    keep(fac_ref, CLOSE + 50, through)
    keep(fac_ref, CLOSE + 75, into)
    own = minus(tail_tail, mm(tail_head, reach))
    upp = mturn(negative(mm(h0m, reach)), -WIDTH)
    low, nxt = through, into
    if STAGES:
        link = shifted(half_before(h3), e)
        low, nxt = mm(through, link), mm(into, link)
    nxt = mturn(nxt, -WIDTH)
    for distance, base in STAGES:
        low, own, nxt, upp = stage(fac_ref, base, low, own, nxt, upp, distance)
    keep(end_ref, 0, low)
    keep(end_ref, 25, own)
    keep(end_ref, 50, nxt)
    keep(end_ref, 75, upp)
    place = 100
    for a in N:
        for b in range(a, 5):
            end_ref[8 * place : 8 * place + 8, :] = turn(h3p[a][b], 1 - WIDTH)
            place += 1
    for number in range(15):
        pack_ref[8 * number : 8 * number + 8, :] = rows_of_last(end_ref, number)


def rhs_kernel(
    jac_ref, step_ref, src_ref, flux_ref, even_ref, odd_ref, fac_ref, part_ref, pack_ref, val_ref, res_ref, end_ref
):
    e = damping
    lane = lax.broadcasted_iota(jnp.int32, (CHUNKS * CELLS, LANES), 1)
    is_even = lax.axis_index("cross") % 2 == 0
    for a in N:
        flux = flux_ref[a].astype(jnp.float32)
        even_swap = even_ref[a].astype(jnp.float32)
        odd_swap = odd_ref[a].astype(jnp.float32)
        after = jnp.where(is_even, even_swap, odd_swap)
        before = jnp.where(is_even, odd_swap, even_swap)
        upper = pltpu.roll(jnp.where(lane < NZ, after, flux), LANES - NZ, axis=1)
        lower = pltpu.roll(jnp.where(lane >= LANES - NZ, before, flux), NZ, axis=1)
        res_ref[a] = src_ref[a].astype(jnp.float32) - 0.5 * (upper - lower)
    r0, r1, r2, r3 = ([res_ref[a, pl.ds(cell, CHUNKS, stride=CELLS), :] for a in N] for cell in range(CELLS))
    h1 = half_jacobian(jac_ref, 1)
    h2 = half_jacobian(jac_ref, 2)
    d1 = diagonal(step_ref, 1)
    d2 = diagonal(step_ref, 2)
    inv = block(fac_ref, 0)
    part = mv(inv, r1)
    x1 = vminus([d2 * value for value in part], mv(inv, mv(shifted(h2, -e), r2)))
    x2 = vplus(mv(shifted(h1, e), part), [d1 * value for value in mv(flipped(inv), r2)])
    keep_vector(val_ref, 0, x1)
    keep_vector(val_ref, 5, x2)
    head = vminus(r0, mv(shifted(h1, -e), x1))
    tail = vplus(r3, mv(shifted(h2, e), x2))
    place = 10
    for distance, base in MERGES:
        latter = (vturn(head, -distance), vturn(tail, -distance))
        inner_tail, inner_head, head, tail = merge_rhs(fac_ref, base, (head, tail), latter)
        keep_vector(val_ref, place, inner_tail)
        keep_vector(val_ref, place + 5, inner_head)
        place += 10
    keep_vector(val_ref, place, mv(block(fac_ref, CLOSE), head))
    own = vminus(tail, mv(block(fac_ref, CLOSE + 50), head))
    nxt = vturn([-value for value in mv(block(fac_ref, CLOSE + 75), head)], -WIDTH)
    for distance, base in STAGES:
        place += 5
        value, own, nxt = stage_rhs(fac_ref, base, own, nxt, distance)
        keep_vector(val_ref, place, value)
    end_ref[...] = jnp.zeros_like(end_ref)
    keep_vector(end_ref, 3, own)
    keep_vector(end_ref, 8, nxt)
    pack_ref[:112, :] = part_ref[:112, :]
    row = lax.broadcasted_iota(jnp.int32, (8, LANES), 0)
    pack_ref[112:120, :] = jnp.where(row < 3, part_ref[112:120, :], rows_of_last(end_ref, 0))
    pack_ref[120:125, :] = rows_of_last(end_ref, 1)[:5]


def solve_kernel(sent_ref, jac_ref, step_ref, fac_ref, val_ref, out_hbm, out_ref, all_ref, red_ref, x_ref, w_ref, sems):
    solve(sent_ref, jac_ref, step_ref, fac_ref, val_ref, out_ref, all_ref, red_ref, x_ref, w_ref)
    copies = [pltpu.make_async_copy(out_ref.at[a], out_hbm.at[a], sems.at[a]) for a in N]
    for copy in copies:
        copy.start()
    for copy in copies:
        copy.wait()


def solve(sent_ref, jac_ref, step_ref, fac_ref, val_ref, out_ref, all_ref, red_ref, x_ref, w_ref):
    e = damping
    for device in range(16):
        all_ref[ROWS * device : ROWS * device + SENT, :] = sent_ref[device]
    row = lax.broadcasted_iota(jnp.int32, (CHUNKS, LANES), 0)

    def packed(parity, number):
        return all_ref[pl.ds(parity * ROWS + number, 8, stride=2 * ROWS), :]

    def packed_block(parity, base):
        return [[packed(parity, base + 5 * a + b) for b in N] for a in N]

    def packed_vector(parity, base):
        return [packed(parity, base + a) for a in N]

    def packed_symmetric(parity, base):
        result = [[None] * 5 for _ in N]
        for a in N:
            for b in range(a, 5):
                result[a][b] = result[b][a] = packed(parity, base)
                base += 1
        return result

    m_even = packed_symmetric(0, 100)
    m_odd = packed_symmetric(1, 100)
    value, (vlow, vupp) = solved(
        plus(packed_block(0, 25), mm(packed_block(1, 50), m_even)),
        vplus(packed_vector(0, 115), packed_vector(1, 120)),
        packed_block(0, 0),
        packed_block(1, 75),
    )
    keep(red_ref, VLOW, vlow)
    keep(red_ref, VUPP, vupp)
    keep_vector(x_ref, 4, value)
    cross = mm(packed_block(1, 0), m_even)
    own = minus(packed_block(1, 25), mm(cross, vupp))
    low = negative(mm(cross, vlow))
    own_rhs = vminus(packed_vector(1, 115), mv(cross, value))
    back = packed_block(0, 75)
    nxt = minus(packed_block(0, 50), mm(back, vlow))
    upp = negative(mm(back, vupp))
    nxt_rhs = vminus(packed_vector(0, 120), mv(back, value))
    first, last = row == 0, row == CHUNKS - 1
    low = mm(low, mturn(m_odd, 1))
    low = [[jnp.where(first, 0.0, low[a][b]) for b in N] for a in N]
    nxt = mm(mturn(nxt, -1), m_odd)
    nxt = [[jnp.where(last, 0.0, nxt[a][b]) for b in N] for a in N]
    upp = [[jnp.where(last, 0.0, turn(upp[a][b], -1)) for b in N] for a in N]
    nxt_rhs = [jnp.where(last, 0.0, turn(nxt_rhs[a], -1)) for a in N]
    for distance in (1, 2, 4):
        value, (vlow, vupp) = solved(plus(own, nxt), vplus(own_rhs, nxt_rhs), low, upp)
        own_rhs = vminus(own_rhs, mv(low, vturn(value, distance)))
        nxt_rhs = vminus(nxt_rhs, mv(upp, vturn(value, -distance)))
        low, own, nxt, upp = next_rows(low, own, nxt, upp, vlow, vupp, distance)
    x = solved(plus(own, nxt), vplus(own_rhs, nxt_rhs))[0]
    w_odd = mv(m_odd, x)
    before = [jnp.where(first, 0.0, turn(w_odd[a], 1)) for a in N]
    x_even = stage_back(red_ref, 0, vector(x_ref, 4), before, x)
    w_even = mv(m_even, x_even)
    position = lax.axis_index("line")
    half, odd = position // 2, position % 2
    is_odd = odd == 1
    for a in N:
        w_ref[8 * a : 8 * a + 8, :] = jnp.where(is_odd, w_even[a], before[a])
        x_ref[8 * a : 8 * a + 8, :] = jnp.where(is_odd, x[a], x_even[a])
    ends = [jnp.broadcast_to(x_ref[pl.ds(8 * a + half, 1), :], (CHUNKS, LANES)) for a in N]
    w = [jnp.broadcast_to(w_ref[pl.ds(8 * a + half, 1), :], (CHUNKS, LANES)) for a in N]

    def neighbour(values, distance):
        return [jnp.where(row < distance, w[a], turn(values[a], distance)) for a in N]

    last = ends
    place = VALUES - 5
    for distance, base in reversed(STAGES):
        found = stage_back(fac_ref, base, vector(val_ref, place), neighbour(last, distance), vturn(last, -distance))
        place -= 5
        chosen = (row % (2 * distance)) == distance - WIDTH
        last = [jnp.where(chosen, found[a], last[a]) for a in N]
    if STAGES:
        w = mv(shifted(half_before(half_jacobian(jac_ref, 3)), e), neighbour(last, WIDTH))
    first = vplus(
        vector(val_ref, place), vminus(mv(block(fac_ref, CLOSE), w), mv(block(fac_ref, CLOSE + 25), last))
    )
    for distance, base in reversed(MERGES):
        place -= 10
        tail, head = merge_back(fac_ref, base, vector(val_ref, place), vector(val_ref, place + 5), first, last)
        latter = (row % (2 * distance)) >= distance
        first = [jnp.where(latter, turn(head[a], distance), first[a]) for a in N]
        last = [jnp.where(latter, turn(last[a], distance), tail[a]) for a in N]
    d1 = diagonal(step_ref, 1)
    d2 = diagonal(step_ref, 2)
    part = mv(block(fac_ref, 25), first)
    x1 = vplus(vplus(vector(val_ref, 0), [d2 * value for value in part]), mv(block(fac_ref, 50), last))
    far = mv(block(fac_ref, 75), last)
    near = mv(shifted(half_jacobian(jac_ref, 1), e), part)
    x2 = vplus(vector(val_ref, 5), vminus(near, [d1 * value for value in far]))
    for a in N:
        out_ref[a, pl.ds(0, CHUNKS, stride=CELLS), :] = first[a]
        out_ref[a, pl.ds(1, CHUNKS, stride=CELLS), :] = x1[a]
        out_ref[a, pl.ds(2, CHUNKS, stride=CELLS), :] = x2[a]
        out_ref[a, pl.ds(3, CHUNKS, stride=CELLS), :] = last[a]


INTERPRET = False


VMEM = pl.BlockSpec(memory_space=pltpu.VMEM)
HBM = pl.BlockSpec(memory_space=pltpu.MemorySpace.HBM)


def kept(shape, dtype=jnp.float32):
    return jax.ShapeDtypeStruct(shape, dtype) if INTERPRET else pltpu.VMEM(shape, dtype)


def inside(values):
    return values if INTERPRET else [pltpu.with_memory_space_constraint(value, pltpu.VMEM) for value in values]


def outside(values):
    return values if INTERPRET else [pltpu.with_memory_space_constraint(value, pltpu.MemorySpace.HBM) for value in values]


def run(kernel, name, outs, args, scratch, far_args=0, far_outs=0):
    return pl.pallas_call(
        kernel,
        out_shape=outs,
        in_specs=[HBM] * far_args + [VMEM] * (len(args) - far_args),
        out_specs=[HBM] * far_outs + [VMEM] * (len(outs) - far_outs),
        scratch_shapes=scratch,
        compiler_params=pltpu.CompilerParams(vmem_limit_bytes=12 << 20),
        interpret=INTERPRET,
        name=name,
    )(*outside(args[:far_args]), *inside(args[far_args:]))


def tiles(count):
    return pltpu.VMEM((8 * count, LANES), jnp.float32)


def shards(jacobian, time_step, source, cross_flux):
    count = lax.axis_size("cross")
    cells = CHUNKS * CELLS
    even_swap, odd_swap = (
        lax.ppermute(
            cross_flux,
            "cross",
            [pair for i in range(start, count - 1, 2) for pair in ((i, i + 1), (i + 1, i))],
        )
        for start in (0, 1)
    )
    jac, step, src, flux, factors, part = run(
        factor_kernel,
        "factor",
        [
            kept((5, 5, cells, LANES)),
            kept((cells, LANES)),
            kept((5, cells, LANES), jnp.bfloat16),
            kept((5, cells, LANES), jnp.bfloat16),
            kept((8 * TILES, LANES)),
            kept((120, LANES)),
        ],
        [jacobian, time_step, source, cross_flux],
        [tiles(120), pltpu.SemaphoreType.DMA((8,))],
        far_args=4,
    )
    packet, values = run(
        rhs_kernel,
        "right_side",
        [kept((SENT, LANES)), kept((8 * VALUES, LANES))],
        [jac, step, src, flux, even_swap, odd_swap, factors, part],
        [pltpu.VMEM((5, cells, LANES), jnp.float32), tiles(16)],
    )
    packets = lax.all_gather(packet, "line", axis=0)
    return run(
        solve_kernel,
        "solve",
        [jax.ShapeDtypeStruct((5, cells, LANES), jnp.float32)],
        [packets, jac, step, factors, values],
        [
            pltpu.VMEM((5, cells, LANES), jnp.float32),
            tiles(2 * ROWS),
            tiles(STAGE),
            tiles(16),
            tiles(5),
            pltpu.SemaphoreType.DMA((5,)),
        ],
        far_outs=1,
    )[0]


def solution(mesh):
    placed = (
        P(None, None, "line", "cross"),
        P("line", "cross"),
        P(None, "line", "cross"),
        P(None, "line", "cross"),
    )
    return jax.shard_map(
        shards, mesh=mesh, in_specs=placed, out_specs=P(None, "line", "cross"), check_vma=False
    )
```

```python
import jax
import jax.numpy as jnp
from jax import lax
from jax.experimental import pallas as pl
from jax.experimental.pallas import tpu as pltpu
from jax.sharding import PartitionSpec as P

NZ = 8
damping = 0.05

CHUNKS = 8
CELLS = 4
LANES = 128
SENT = 125
ROWS = 128
INV, LOW, UPP, VLOW, VUPP = (25 * k for k in range(5))
STAGE = 125
N = range(5)


def tile(ref, number):
    return ref[8 * number : 8 * number + 8, :]


def block(ref, base):
    return [[tile(ref, base + 5 * a + b) for b in N] for a in N]


def vector(ref, base):
    return [tile(ref, base + a) for a in N]


def keep(ref, base, matrix):
    for a in N:
        for b in N:
            ref[8 * (base + 5 * a + b) : 8 * (base + 5 * a + b) + 8, :] = matrix[a][b]


def keep_vector(ref, base, values):
    for a in N:
        ref[8 * (base + a) : 8 * (base + a) + 8, :] = values[a]


def total(terms):
    result = terms[0]
    for term in terms[1:]:
        result = result + term
    return result


def mm(left, right):
    return [[total([left[a][k] * right[k][b] for k in N]) for b in N] for a in N]


def mv(left, right):
    return [total([left[a][k] * right[k] for k in N]) for a in N]


def plus(left, right):
    return [[left[a][b] + right[a][b] for b in N] for a in N]


def minus(left, right):
    return [[left[a][b] - right[a][b] for b in N] for a in N]


def negative(matrix):
    return [[-matrix[a][b] for b in N] for a in N]


def vplus(left, right):
    return [left[a] + right[a] for a in N]


def vminus(left, right):
    return [left[a] - right[a] for a in N]


def scaled(factor, matrix):
    return [[factor * matrix[a][b] for b in N] for a in N]


def shifted(matrix, amount):
    return [[matrix[a][b] + amount if a == b else matrix[a][b] for b in N] for a in N]


def turn(value, count):
    return pltpu.roll(value, count % CHUNKS, axis=0)


def flipped(matrix):
    return [[matrix[b][a] for b in N] for a in N]


def mturn(matrix, count):
    return [[turn(matrix[a][b], count) for b in N] for a in N]


def vturn(values, count):
    return [turn(values[a], count) for a in N]


def inverse_and_solved(matrix, *sides):
    m = [list(row) + [side[a][b] for side in sides for b in N] for a, row in enumerate(matrix)]
    width = len(m[0])
    for k in N:
        pivot = 1.0 / m[k][k]
        for b in range(width):
            m[k][b] = pivot if b == k else m[k][b] * pivot
        for a in N:
            if a != k:
                factor = m[a][k]
                for b in range(width):
                    m[a][b] = -factor * pivot if b == k else m[a][b] - factor * m[k][b]
    return [[row[at : at + 5] for row in m] for at in range(0, width, 5)]


def solved(matrix, values, *sides):
    m = [list(row) + [values[a]] + [side[a][b] for side in sides for b in N] for a, row in enumerate(matrix)]
    width = len(m[0])
    for k in N:
        pivot = 1.0 / m[k][k]
        for b in range(k + 1, width):
            m[k][b] = m[k][b] * pivot
        for a in N:
            if a != k:
                for b in range(k + 1, width):
                    m[a][b] = m[a][b] - m[a][k] * m[k][b]
    return [row[5] for row in m], [[row[at : at + 5] for row in m] for at in range(6, width, 5)]


def half_jacobian(jac_ref, cell):
    half = [[None] * 5 for _ in N]
    for a in N:
        for b in range(a, 5):
            half[a][b] = half[b][a] = 0.5 * jac_ref[a, b, pl.ds(cell, CHUNKS, stride=CELLS), :]
    return half


def half_before(half_last):
    first = lax.broadcasted_iota(jnp.int32, (CHUNKS, LANES), 0) == 0
    result = [[None] * 5 for _ in N]
    for a in N:
        for b in range(a, 5):
            outside = 1.0 - damping if a == b else 0.0
            result[a][b] = result[b][a] = jnp.where(first, outside, turn(half_last[a][b], 1))
    return result


def diagonal(step_ref, cell):
    return 1.0 / step_ref[pl.ds(cell, CHUNKS, stride=CELLS), :] + 2.0 * damping


def next_rows(low, own, nxt, upp, vlow, vupp, distance):
    vlow_before, vupp_before = mturn(vlow, distance), mturn(vupp, distance)
    vlow_after, vupp_after = vlow_before, vupp_before
    if 2 * distance != CHUNKS:
        vlow_after, vupp_after = mturn(vlow, -distance), mturn(vupp, -distance)
    return (
        negative(mm(low, vlow_before)),
        minus(own, mm(low, vupp_before)),
        minus(nxt, mm(upp, vlow_after)),
        negative(mm(upp, vupp_after)),
    )


def stage(fac_ref, base, low, own, nxt, upp, distance):
    inv, vlow, vupp = inverse_and_solved(plus(own, nxt), low, upp)
    keep(fac_ref, base + INV, inv)
    keep(fac_ref, base + LOW, low)
    keep(fac_ref, base + UPP, upp)
    keep(fac_ref, base + VLOW, vlow)
    keep(fac_ref, base + VUPP, vupp)
    return next_rows(low, own, nxt, upp, vlow, vupp, distance)


def stage_rhs(fac_ref, base, own, nxt, distance):
    value = mv(block(fac_ref, base + INV), vplus(own, nxt))
    own = vminus(own, mv(block(fac_ref, base + LOW), vturn(value, distance)))
    nxt = vminus(nxt, mv(block(fac_ref, base + UPP), vturn(value, -distance)))
    return value, own, nxt


def stage_back(fac_ref, base, value, before, after):
    return vminus(
        vminus(value, mv(block(fac_ref, base + VLOW), before)), mv(block(fac_ref, base + VUPP), after)
    )


def merge(fac_ref, base, former, latter, upp, low):
    head_head, head_tail, tail_head, tail_tail = former
    inv_head, carry, reach = inverse_and_solved(latter[0], low, latter[1])
    inv_tail, tail_by_head, tail_by_tail = inverse_and_solved(
        plus(tail_tail, mm(upp, carry)), tail_head, mm(upp, reach)
    )
    head_by_head = mm(carry, tail_by_head)
    head_by_tail = minus(reach, mm(carry, tail_by_tail))
    for number, kept in enumerate(
        (
            inv_head,
            carry,
            inv_tail,
            upp,
            head_tail,
            latter[2],
            tail_by_head,
            tail_by_tail,
            head_by_head,
            head_by_tail,
        )
    ):
        keep(fac_ref, base + 25 * number, kept)
    return (
        minus(head_head, mm(head_tail, tail_by_head)),
        mm(head_tail, tail_by_tail),
        negative(mm(latter[2], head_by_head)),
        minus(latter[3], mm(latter[2], head_by_tail)),
    )


def merge_rhs(fac_ref, base, former, latter):
    head = mv(block(fac_ref, base), latter[0])
    tail = mv(block(fac_ref, base + 50), vminus(former[1], mv(block(fac_ref, base + 75), head)))
    head = vplus(head, mv(block(fac_ref, base + 25), tail))
    return (
        tail,
        head,
        vminus(former[0], mv(block(fac_ref, base + 100), tail)),
        vminus(latter[1], mv(block(fac_ref, base + 125), head)),
    )


def merge_back(fac_ref, base, tail, head, first, last):
    tail = vplus(
        vminus(tail, mv(block(fac_ref, base + 150), first)), mv(block(fac_ref, base + 175), last)
    )
    head = vminus(
        vminus(head, mv(block(fac_ref, base + 200), first)), mv(block(fac_ref, base + 225), last)
    )
    return tail, head


def rows_of_last(ref, group):
    return ref[pl.ds(64 * group + CHUNKS - WIDTH, 8, stride=8), :]


WIDTH = 2
MERGES = tuple((1 << k, 100 + 250 * k) for k in range(WIDTH.bit_length() - 1))
CLOSE = 100 + 250 * len(MERGES)
STAGES = tuple((WIDTH << k, CLOSE + 100 + 125 * k) for k in range((CHUNKS // WIDTH).bit_length() - 1))
TILES = CLOSE + 100 + 125 * len(STAGES)
VALUES = 15 + 10 * len(MERGES) + 5 * len(STAGES)


def factor_kernel(
    jac_hbm, step_hbm, src_hbm, flux_hbm, jac_ref, step_ref, src_ref, flux_ref, fac_ref, pack_ref, end_ref, sems
):
    needed = [pltpu.make_async_copy(jac_hbm.at[a, a:], jac_ref.at[a, a:], sems.at[a]) for a in N]
    needed.append(pltpu.make_async_copy(step_hbm, step_ref, sems.at[5]))
    later = [
        pltpu.make_async_copy(src_hbm, src_ref, sems.at[6]),
        pltpu.make_async_copy(flux_hbm, flux_ref, sems.at[7]),
    ]
    for copy in needed + later:
        copy.start()
    for copy in needed:
        copy.wait()
    factor(jac_ref, step_ref, fac_ref, pack_ref, end_ref)
    for copy in later:
        copy.wait()


def factor(jac_ref, step_ref, fac_ref, pack_ref, end_ref):
    e = damping
    h0 = half_jacobian(jac_ref, 0)
    h1 = half_jacobian(jac_ref, 1)
    h2 = half_jacobian(jac_ref, 2)
    h3 = half_jacobian(jac_ref, 3)
    d1 = diagonal(step_ref, 1)
    d2 = diagonal(step_ref, 2)
    h0p, h1p, h2p, h3p = shifted(h0, e), shifted(h1, e), shifted(h2, e), shifted(h3, e)
    h0m, h1m, h2m, h3m = shifted(h0, -e), shifted(h1, -e), shifted(h2, -e), shifted(h3, -e)
    inv, by_low, by_upp = inverse_and_solved(shifted(mm(h2m, h1p), d1 * d2), h0p, mm(h2m, h3m))
    by_end = mm(flipped(inv), h3m)
    pair = mm(h2p, h1p)
    group = (
        shifted(mm(h1m, scaled(d2, by_low)), diagonal(step_ref, 0)),
        mm(h1m, by_upp),
        negative(mm(pair, by_low)),
        shifted(mm(scaled(d1, h2p), by_end), diagonal(step_ref, 3)),
    )
    keep(fac_ref, 0, inv)
    keep(fac_ref, 25, by_low)
    keep(fac_ref, 50, by_upp)
    keep(fac_ref, 75, by_end)
    for distance, base in MERGES:
        latter = tuple(mturn(part, -distance) for part in group)
        group = merge(fac_ref, base, group, latter, mturn(h0m, -distance), mturn(h3p, 1 - distance))
    head_head, head_tail, tail_head, tail_tail = group
    inv, reach = inverse_and_solved(head_head, head_tail)
    through = mm(tail_head, inv)
    into = mm(h0m, inv)
    keep(fac_ref, CLOSE, inv)
    keep(fac_ref, CLOSE + 25, reach)
    keep(fac_ref, CLOSE + 50, through)
    keep(fac_ref, CLOSE + 75, into)
    own = minus(tail_tail, mm(tail_head, reach))
    upp = mturn(negative(mm(h0m, reach)), -WIDTH)
    low, nxt = through, into
    if STAGES:
        link = shifted(half_before(h3), e)
        low, nxt = mm(through, link), mm(into, link)
    nxt = mturn(nxt, -WIDTH)
    for distance, base in STAGES:
        low, own, nxt, upp = stage(fac_ref, base, low, own, nxt, upp, distance)
    keep(end_ref, 0, low)
    keep(end_ref, 25, own)
    keep(end_ref, 50, nxt)
    keep(end_ref, 75, upp)
    place = 100
    for a in N:
        for b in range(a, 5):
            end_ref[8 * place : 8 * place + 8, :] = turn(h3p[a][b], 1 - WIDTH)
            place += 1
    for number in range(15):
        pack_ref[8 * number : 8 * number + 8, :] = rows_of_last(end_ref, number)


def rhs_kernel(
    jac_ref, step_ref, src_ref, flux_ref, even_ref, odd_ref, fac_ref, part_ref, pack_ref, val_ref, res_ref, end_ref
):
    e = damping
    lane = lax.broadcasted_iota(jnp.int32, (CHUNKS * CELLS, LANES), 1)
    is_even = lax.axis_index("cross") % 2 == 0
    for a in N:
        flux = flux_ref[a].astype(jnp.float32)
        even_swap = even_ref[a].astype(jnp.float32)
        odd_swap = odd_ref[a].astype(jnp.float32)
        after = jnp.where(is_even, even_swap, odd_swap)
        before = jnp.where(is_even, odd_swap, even_swap)
        upper = pltpu.roll(jnp.where(lane < NZ, after, flux), LANES - NZ, axis=1)
        lower = pltpu.roll(jnp.where(lane >= LANES - NZ, before, flux), NZ, axis=1)
        res_ref[a] = src_ref[a].astype(jnp.float32) - 0.5 * (upper - lower)
    r0, r1, r2, r3 = ([res_ref[a, pl.ds(cell, CHUNKS, stride=CELLS), :] for a in N] for cell in range(CELLS))
    h1 = half_jacobian(jac_ref, 1)
    h2 = half_jacobian(jac_ref, 2)
    d1 = diagonal(step_ref, 1)
    d2 = diagonal(step_ref, 2)
    inv = block(fac_ref, 0)
    part = mv(inv, r1)
    x1 = vminus([d2 * value for value in part], mv(inv, mv(shifted(h2, -e), r2)))
    x2 = vplus(mv(shifted(h1, e), part), [d1 * value for value in mv(flipped(inv), r2)])
    keep_vector(val_ref, 0, x1)
    keep_vector(val_ref, 5, x2)
    head = vminus(r0, mv(shifted(h1, -e), x1))
    tail = vplus(r3, mv(shifted(h2, e), x2))
    place = 10
    for distance, base in MERGES:
        latter = (vturn(head, -distance), vturn(tail, -distance))
        inner_tail, inner_head, head, tail = merge_rhs(fac_ref, base, (head, tail), latter)
        keep_vector(val_ref, place, inner_tail)
        keep_vector(val_ref, place + 5, inner_head)
        place += 10
    keep_vector(val_ref, place, mv(block(fac_ref, CLOSE), head))
    own = vminus(tail, mv(block(fac_ref, CLOSE + 50), head))
    nxt = vturn([-value for value in mv(block(fac_ref, CLOSE + 75), head)], -WIDTH)
    for distance, base in STAGES:
        place += 5
        value, own, nxt = stage_rhs(fac_ref, base, own, nxt, distance)
        keep_vector(val_ref, place, value)
    end_ref[...] = jnp.zeros_like(end_ref)
    keep_vector(end_ref, 3, own)
    keep_vector(end_ref, 8, nxt)
    pack_ref[:112, :] = part_ref[:112, :]
    row = lax.broadcasted_iota(jnp.int32, (8, LANES), 0)
    pack_ref[112:120, :] = jnp.where(row < 3, part_ref[112:120, :], rows_of_last(end_ref, 0))
    pack_ref[120:125, :] = rows_of_last(end_ref, 1)[:5]


def solve_kernel(sent_ref, jac_ref, step_ref, fac_ref, val_ref, out_ref, all_ref, red_ref, x_ref, w_ref):
    e = damping
    for device in range(16):
        all_ref[ROWS * device : ROWS * device + SENT, :] = sent_ref[device]
    row = lax.broadcasted_iota(jnp.int32, (CHUNKS, LANES), 0)

    def packed(parity, number):
        return all_ref[pl.ds(parity * ROWS + number, 8, stride=2 * ROWS), :]

    def packed_block(parity, base):
        return [[packed(parity, base + 5 * a + b) for b in N] for a in N]

    def packed_vector(parity, base):
        return [packed(parity, base + a) for a in N]

    def packed_symmetric(parity, base):
        result = [[None] * 5 for _ in N]
        for a in N:
            for b in range(a, 5):
                result[a][b] = result[b][a] = packed(parity, base)
                base += 1
        return result

    m_even = packed_symmetric(0, 100)
    m_odd = packed_symmetric(1, 100)
    value, (vlow, vupp) = solved(
        plus(packed_block(0, 25), mm(packed_block(1, 50), m_even)),
        vplus(packed_vector(0, 115), packed_vector(1, 120)),
        packed_block(0, 0),
        packed_block(1, 75),
    )
    keep(red_ref, VLOW, vlow)
    keep(red_ref, VUPP, vupp)
    keep_vector(x_ref, 4, value)
    cross = mm(packed_block(1, 0), m_even)
    own = minus(packed_block(1, 25), mm(cross, vupp))
    low = negative(mm(cross, vlow))
    own_rhs = vminus(packed_vector(1, 115), mv(cross, value))
    back = packed_block(0, 75)
    nxt = minus(packed_block(0, 50), mm(back, vlow))
    upp = negative(mm(back, vupp))
    nxt_rhs = vminus(packed_vector(0, 120), mv(back, value))
    first, last = row == 0, row == CHUNKS - 1
    low = mm(low, mturn(m_odd, 1))
    low = [[jnp.where(first, 0.0, low[a][b]) for b in N] for a in N]
    nxt = mm(mturn(nxt, -1), m_odd)
    nxt = [[jnp.where(last, 0.0, nxt[a][b]) for b in N] for a in N]
    upp = [[jnp.where(last, 0.0, turn(upp[a][b], -1)) for b in N] for a in N]
    nxt_rhs = [jnp.where(last, 0.0, turn(nxt_rhs[a], -1)) for a in N]
    for distance in (1, 2, 4):
        value, (vlow, vupp) = solved(plus(own, nxt), vplus(own_rhs, nxt_rhs), low, upp)
        own_rhs = vminus(own_rhs, mv(low, vturn(value, distance)))
        nxt_rhs = vminus(nxt_rhs, mv(upp, vturn(value, -distance)))
        low, own, nxt, upp = next_rows(low, own, nxt, upp, vlow, vupp, distance)
    x = solved(plus(own, nxt), vplus(own_rhs, nxt_rhs))[0]
    w_odd = mv(m_odd, x)
    before = [jnp.where(first, 0.0, turn(w_odd[a], 1)) for a in N]
    x_even = stage_back(red_ref, 0, vector(x_ref, 4), before, x)
    w_even = mv(m_even, x_even)
    position = lax.axis_index("line")
    half, odd = position // 2, position % 2
    is_odd = odd == 1
    for a in N:
        w_ref[8 * a : 8 * a + 8, :] = jnp.where(is_odd, w_even[a], before[a])
        x_ref[8 * a : 8 * a + 8, :] = jnp.where(is_odd, x[a], x_even[a])
    ends = [jnp.broadcast_to(x_ref[pl.ds(8 * a + half, 1), :], (CHUNKS, LANES)) for a in N]
    w = [jnp.broadcast_to(w_ref[pl.ds(8 * a + half, 1), :], (CHUNKS, LANES)) for a in N]

    def neighbour(values, distance):
        return [jnp.where(row < distance, w[a], turn(values[a], distance)) for a in N]

    last = ends
    place = VALUES - 5
    for distance, base in reversed(STAGES):
        found = stage_back(fac_ref, base, vector(val_ref, place), neighbour(last, distance), vturn(last, -distance))
        place -= 5
        chosen = (row % (2 * distance)) == distance - WIDTH
        last = [jnp.where(chosen, found[a], last[a]) for a in N]
    if STAGES:
        w = mv(shifted(half_before(half_jacobian(jac_ref, 3)), e), neighbour(last, WIDTH))
    first = vplus(
        vector(val_ref, place), vminus(mv(block(fac_ref, CLOSE), w), mv(block(fac_ref, CLOSE + 25), last))
    )
    for distance, base in reversed(MERGES):
        place -= 10
        tail, head = merge_back(fac_ref, base, vector(val_ref, place), vector(val_ref, place + 5), first, last)
        latter = (row % (2 * distance)) >= distance
        first = [jnp.where(latter, turn(head[a], distance), first[a]) for a in N]
        last = [jnp.where(latter, turn(last[a], distance), tail[a]) for a in N]
    d1 = diagonal(step_ref, 1)
    d2 = diagonal(step_ref, 2)
    part = mv(block(fac_ref, 25), first)
    x1 = vplus(vplus(vector(val_ref, 0), [d2 * value for value in part]), mv(block(fac_ref, 50), last))
    far = mv(block(fac_ref, 75), last)
    near = mv(shifted(half_jacobian(jac_ref, 1), e), part)
    x2 = vplus(vector(val_ref, 5), vminus(near, [d1 * value for value in far]))
    for a in N:
        out_ref[a, pl.ds(0, CHUNKS, stride=CELLS), :] = first[a]
        out_ref[a, pl.ds(1, CHUNKS, stride=CELLS), :] = x1[a]
        out_ref[a, pl.ds(2, CHUNKS, stride=CELLS), :] = x2[a]
        out_ref[a, pl.ds(3, CHUNKS, stride=CELLS), :] = last[a]


INTERPRET = False


VMEM = pl.BlockSpec(memory_space=pltpu.VMEM)
HBM = pl.BlockSpec(memory_space=pltpu.MemorySpace.HBM)


def kept(shape, dtype=jnp.float32):
    return jax.ShapeDtypeStruct(shape, dtype) if INTERPRET else pltpu.VMEM(shape, dtype)


def inside(values):
    return values if INTERPRET else [pltpu.with_memory_space_constraint(value, pltpu.VMEM) for value in values]


def outside(values):
    return values if INTERPRET else [pltpu.with_memory_space_constraint(value, pltpu.MemorySpace.HBM) for value in values]


def run(kernel, name, outs, args, scratch, far_args=0, far_outs=0):
    return pl.pallas_call(
        kernel,
        out_shape=outs,
        in_specs=[HBM] * far_args + [VMEM] * (len(args) - far_args),
        out_specs=[HBM] * far_outs + [VMEM] * (len(outs) - far_outs),
        scratch_shapes=scratch,
        compiler_params=pltpu.CompilerParams(vmem_limit_bytes=12 << 20),
        interpret=INTERPRET,
        name=name,
    )(*outside(args[:far_args]), *inside(args[far_args:]))


def tiles(count):
    return pltpu.VMEM((8 * count, LANES), jnp.float32)


def shards(jacobian, time_step, source, cross_flux):
    count = lax.axis_size("cross")
    cells = CHUNKS * CELLS
    even_swap, odd_swap = (
        lax.ppermute(
            cross_flux,
            "cross",
            [pair for i in range(start, count - 1, 2) for pair in ((i, i + 1), (i + 1, i))],
        )
        for start in (0, 1)
    )
    jac, step, src, flux, factors, part = run(
        factor_kernel,
        "factor",
        [
            kept((5, 5, cells, LANES)),
            kept((cells, LANES)),
            kept((5, cells, LANES), jnp.bfloat16),
            kept((5, cells, LANES), jnp.bfloat16),
            kept((8 * TILES, LANES)),
            kept((120, LANES)),
        ],
        [jacobian, time_step, source, cross_flux],
        [tiles(120), pltpu.SemaphoreType.DMA((8,))],
        far_args=4,
    )
    packet, values = run(
        rhs_kernel,
        "right_side",
        [kept((SENT, LANES)), kept((8 * VALUES, LANES))],
        [jac, step, src, flux, even_swap, odd_swap, factors, part],
        [pltpu.VMEM((5, cells, LANES), jnp.float32), tiles(16)],
    )
    packets = lax.all_gather(packet, "line", axis=0)
    return run(
        solve_kernel,
        "solve",
        [kept((5, cells, LANES))],
        [packets, jac, step, factors, values],
        [
            tiles(2 * ROWS),
            tiles(STAGE),
            tiles(16),
            tiles(5),
        ],
    )[0]


def solution(mesh):
    placed = (
        P(None, None, "line", "cross"),
        P("line", "cross"),
        P(None, "line", "cross"),
        P(None, "line", "cross"),
    )
    return jax.shard_map(
        shards, mesh=mesh, in_specs=placed, out_specs=P(None, "line", "cross"), check_vma=False
    )
```

```python
import jax
import jax.numpy as jnp
from jax import lax
from jax.experimental import pallas as pl
from jax.experimental.pallas import tpu as pltpu
from jax.sharding import PartitionSpec as P

NZ = 8
damping = 0.05

CHUNKS = 8
CELLS = 4
LANES = 128
SENT = 125
ROWS = 128
INV, LOW, UPP, VLOW, VUPP = (25 * k for k in range(5))
STAGE = 125
N = range(5)


def tile(ref, number):
    return ref[8 * number : 8 * number + 8, :]


def block(ref, base):
    return [[tile(ref, base + 5 * a + b) for b in N] for a in N]


def vector(ref, base):
    return [tile(ref, base + a) for a in N]


def keep(ref, base, matrix):
    for a in N:
        for b in N:
            ref[8 * (base + 5 * a + b) : 8 * (base + 5 * a + b) + 8, :] = matrix[a][b]


def keep_vector(ref, base, values):
    for a in N:
        ref[8 * (base + a) : 8 * (base + a) + 8, :] = values[a]


def total(terms):
    result = terms[0]
    for term in terms[1:]:
        result = result + term
    return result


def mm(left, right):
    return [[total([left[a][k] * right[k][b] for k in N]) for b in N] for a in N]


def mv(left, right):
    return [total([left[a][k] * right[k] for k in N]) for a in N]


def plus(left, right):
    return [[left[a][b] + right[a][b] for b in N] for a in N]


def minus(left, right):
    return [[left[a][b] - right[a][b] for b in N] for a in N]


def negative(matrix):
    return [[-matrix[a][b] for b in N] for a in N]


def vplus(left, right):
    return [left[a] + right[a] for a in N]


def vminus(left, right):
    return [left[a] - right[a] for a in N]


def scaled(factor, matrix):
    return [[factor * matrix[a][b] for b in N] for a in N]


def shifted(matrix, amount):
    return [[matrix[a][b] + amount if a == b else matrix[a][b] for b in N] for a in N]


def turn(value, count):
    return pltpu.roll(value, count % CHUNKS, axis=0)


def flipped(matrix):
    return [[matrix[b][a] for b in N] for a in N]


def mturn(matrix, count):
    return [[turn(matrix[a][b], count) for b in N] for a in N]


def vturn(values, count):
    return [turn(values[a], count) for a in N]


def inverse_and_solved(matrix, *sides):
    m = [list(row) + [side[a][b] for side in sides for b in N] for a, row in enumerate(matrix)]
    width = len(m[0])
    for k in N:
        pivot = 1.0 / m[k][k]
        for b in range(width):
            m[k][b] = pivot if b == k else m[k][b] * pivot
        for a in N:
            if a != k:
                factor = m[a][k]
                for b in range(width):
                    m[a][b] = -factor * pivot if b == k else m[a][b] - factor * m[k][b]
    return [[row[at : at + 5] for row in m] for at in range(0, width, 5)]


def solved(matrix, values, *sides):
    m = [list(row) + [values[a]] + [side[a][b] for side in sides for b in N] for a, row in enumerate(matrix)]
    width = len(m[0])
    for k in N:
        pivot = 1.0 / m[k][k]
        for b in range(k + 1, width):
            m[k][b] = m[k][b] * pivot
        for a in N:
            if a != k:
                for b in range(k + 1, width):
                    m[a][b] = m[a][b] - m[a][k] * m[k][b]
    return [row[5] for row in m], [[row[at : at + 5] for row in m] for at in range(6, width, 5)]


def half_jacobian(jac_ref, cell):
    half = [[None] * 5 for _ in N]
    for a in N:
        for b in range(a, 5):
            half[a][b] = half[b][a] = 0.5 * jac_ref[a, b, pl.ds(cell, CHUNKS, stride=CELLS), :]
    return half


def half_before(half_last):
    first = lax.broadcasted_iota(jnp.int32, (CHUNKS, LANES), 0) == 0
    result = [[None] * 5 for _ in N]
    for a in N:
        for b in range(a, 5):
            outside = 1.0 - damping if a == b else 0.0
            result[a][b] = result[b][a] = jnp.where(first, outside, turn(half_last[a][b], 1))
    return result


def diagonal(step_ref, cell):
    return 1.0 / step_ref[pl.ds(cell, CHUNKS, stride=CELLS), :] + 2.0 * damping


def next_rows(low, own, nxt, upp, vlow, vupp, distance):
    vlow_before, vupp_before = mturn(vlow, distance), mturn(vupp, distance)
    vlow_after, vupp_after = vlow_before, vupp_before
    if 2 * distance != CHUNKS:
        vlow_after, vupp_after = mturn(vlow, -distance), mturn(vupp, -distance)
    return (
        negative(mm(low, vlow_before)),
        minus(own, mm(low, vupp_before)),
        minus(nxt, mm(upp, vlow_after)),
        negative(mm(upp, vupp_after)),
    )


def stage(fac_ref, base, low, own, nxt, upp, distance):
    inv, vlow, vupp = inverse_and_solved(plus(own, nxt), low, upp)
    keep(fac_ref, base + INV, inv)
    keep(fac_ref, base + LOW, low)
    keep(fac_ref, base + UPP, upp)
    keep(fac_ref, base + VLOW, vlow)
    keep(fac_ref, base + VUPP, vupp)
    return next_rows(low, own, nxt, upp, vlow, vupp, distance)


def stage_rhs(fac_ref, base, own, nxt, distance):
    value = mv(block(fac_ref, base + INV), vplus(own, nxt))
    own = vminus(own, mv(block(fac_ref, base + LOW), vturn(value, distance)))
    nxt = vminus(nxt, mv(block(fac_ref, base + UPP), vturn(value, -distance)))
    return value, own, nxt


def stage_back(fac_ref, base, value, before, after):
    return vminus(
        vminus(value, mv(block(fac_ref, base + VLOW), before)), mv(block(fac_ref, base + VUPP), after)
    )


def merge(fac_ref, base, former, latter, upp, low):
    head_head, head_tail, tail_head, tail_tail = former
    inv_head, carry, reach = inverse_and_solved(latter[0], low, latter[1])
    inv_tail, tail_by_head, tail_by_tail = inverse_and_solved(
        plus(tail_tail, mm(upp, carry)), tail_head, mm(upp, reach)
    )
    head_by_head = mm(carry, tail_by_head)
    head_by_tail = minus(reach, mm(carry, tail_by_tail))
    for number, kept in enumerate(
        (
            inv_head,
            carry,
            inv_tail,
            upp,
            head_tail,
            latter[2],
            tail_by_head,
            tail_by_tail,
            head_by_head,
            head_by_tail,
        )
    ):
        keep(fac_ref, base + 25 * number, kept)
    return (
        minus(head_head, mm(head_tail, tail_by_head)),
        mm(head_tail, tail_by_tail),
        negative(mm(latter[2], head_by_head)),
        minus(latter[3], mm(latter[2], head_by_tail)),
    )


def merge_rhs(fac_ref, base, former, latter):
    head = mv(block(fac_ref, base), latter[0])
    tail = mv(block(fac_ref, base + 50), vminus(former[1], mv(block(fac_ref, base + 75), head)))
    head = vplus(head, mv(block(fac_ref, base + 25), tail))
    return (
        tail,
        head,
        vminus(former[0], mv(block(fac_ref, base + 100), tail)),
        vminus(latter[1], mv(block(fac_ref, base + 125), head)),
    )


def merge_back(fac_ref, base, tail, head, first, last):
    tail = vplus(
        vminus(tail, mv(block(fac_ref, base + 150), first)), mv(block(fac_ref, base + 175), last)
    )
    head = vminus(
        vminus(head, mv(block(fac_ref, base + 200), first)), mv(block(fac_ref, base + 225), last)
    )
    return tail, head


def rows_of_last(ref, group):
    return ref[pl.ds(64 * group + CHUNKS - WIDTH, 8, stride=8), :]


WIDTH = 1
MERGES = tuple((1 << k, 100 + 250 * k) for k in range(WIDTH.bit_length() - 1))
CLOSE = 100 + 250 * len(MERGES)
STAGES = tuple((WIDTH << k, CLOSE + 100 + 125 * k) for k in range((CHUNKS // WIDTH).bit_length() - 1))
TILES = CLOSE + 100 + 125 * len(STAGES)
VALUES = 15 + 10 * len(MERGES) + 5 * len(STAGES)


def factor_kernel(
    jac_hbm, step_hbm, src_hbm, flux_hbm, jac_ref, step_ref, src_ref, flux_ref, fac_ref, pack_ref, end_ref, sems
):
    needed = [pltpu.make_async_copy(jac_hbm.at[a, a:], jac_ref.at[a, a:], sems.at[a]) for a in N]
    needed.append(pltpu.make_async_copy(step_hbm, step_ref, sems.at[5]))
    later = [
        pltpu.make_async_copy(src_hbm, src_ref, sems.at[6]),
        pltpu.make_async_copy(flux_hbm, flux_ref, sems.at[7]),
    ]
    for copy in needed + later:
        copy.start()
    for copy in needed:
        copy.wait()
    factor(jac_ref, step_ref, fac_ref, pack_ref, end_ref)
    for copy in later:
        copy.wait()


def factor(jac_ref, step_ref, fac_ref, pack_ref, end_ref):
    e = damping
    h0 = half_jacobian(jac_ref, 0)
    h1 = half_jacobian(jac_ref, 1)
    h2 = half_jacobian(jac_ref, 2)
    h3 = half_jacobian(jac_ref, 3)
    d1 = diagonal(step_ref, 1)
    d2 = diagonal(step_ref, 2)
    h0p, h1p, h2p, h3p = shifted(h0, e), shifted(h1, e), shifted(h2, e), shifted(h3, e)
    h0m, h1m, h2m, h3m = shifted(h0, -e), shifted(h1, -e), shifted(h2, -e), shifted(h3, -e)
    inv, by_low, by_upp = inverse_and_solved(shifted(mm(h2m, h1p), d1 * d2), h0p, mm(h2m, h3m))
    by_end = mm(flipped(inv), h3m)
    pair = mm(h2p, h1p)
    group = (
        shifted(mm(h1m, scaled(d2, by_low)), diagonal(step_ref, 0)),
        mm(h1m, by_upp),
        negative(mm(pair, by_low)),
        shifted(mm(scaled(d1, h2p), by_end), diagonal(step_ref, 3)),
    )
    keep(fac_ref, 0, inv)
    keep(fac_ref, 25, by_low)
    keep(fac_ref, 50, by_upp)
    keep(fac_ref, 75, by_end)
    for distance, base in MERGES:
        latter = tuple(mturn(part, -distance) for part in group)
        group = merge(fac_ref, base, group, latter, mturn(h0m, -distance), mturn(h3p, 1 - distance))
    head_head, head_tail, tail_head, tail_tail = group
    inv, reach = inverse_and_solved(head_head, head_tail)
    through = mm(tail_head, inv)
    into = mm(h0m, inv)
    keep(fac_ref, CLOSE, inv)
    keep(fac_ref, CLOSE + 25, reach)
    keep(fac_ref, CLOSE + 50, through)
    keep(fac_ref, CLOSE + 75, into)
    own = minus(tail_tail, mm(tail_head, reach))
    upp = mturn(negative(mm(h0m, reach)), -WIDTH)
    low, nxt = through, into
    if STAGES:
        link = shifted(half_before(h3), e)
        low, nxt = mm(through, link), mm(into, link)
    nxt = mturn(nxt, -WIDTH)
    for distance, base in STAGES:
        low, own, nxt, upp = stage(fac_ref, base, low, own, nxt, upp, distance)
    keep(end_ref, 0, low)
    keep(end_ref, 25, own)
    keep(end_ref, 50, nxt)
    keep(end_ref, 75, upp)
    place = 100
    for a in N:
        for b in range(a, 5):
            end_ref[8 * place : 8 * place + 8, :] = turn(h3p[a][b], 1 - WIDTH)
            place += 1
    for number in range(15):
        pack_ref[8 * number : 8 * number + 8, :] = rows_of_last(end_ref, number)


def rhs_kernel(
    jac_ref, step_ref, src_ref, flux_ref, even_ref, odd_ref, fac_ref, part_ref, pack_ref, val_ref, res_ref, end_ref
):
    e = damping
    lane = lax.broadcasted_iota(jnp.int32, (CHUNKS * CELLS, LANES), 1)
    is_even = lax.axis_index("cross") % 2 == 0
    for a in N:
        flux = flux_ref[a].astype(jnp.float32)
        even_swap = even_ref[a].astype(jnp.float32)
        odd_swap = odd_ref[a].astype(jnp.float32)
        after = jnp.where(is_even, even_swap, odd_swap)
        before = jnp.where(is_even, odd_swap, even_swap)
        upper = pltpu.roll(jnp.where(lane < NZ, after, flux), LANES - NZ, axis=1)
        lower = pltpu.roll(jnp.where(lane >= LANES - NZ, before, flux), NZ, axis=1)
        res_ref[a] = src_ref[a].astype(jnp.float32) - 0.5 * (upper - lower)
    r0, r1, r2, r3 = ([res_ref[a, pl.ds(cell, CHUNKS, stride=CELLS), :] for a in N] for cell in range(CELLS))
    h1 = half_jacobian(jac_ref, 1)
    h2 = half_jacobian(jac_ref, 2)
    d1 = diagonal(step_ref, 1)
    d2 = diagonal(step_ref, 2)
    inv = block(fac_ref, 0)
    part = mv(inv, r1)
    x1 = vminus([d2 * value for value in part], mv(inv, mv(shifted(h2, -e), r2)))
    x2 = vplus(mv(shifted(h1, e), part), [d1 * value for value in mv(flipped(inv), r2)])
    keep_vector(val_ref, 0, x1)
    keep_vector(val_ref, 5, x2)
    head = vminus(r0, mv(shifted(h1, -e), x1))
    tail = vplus(r3, mv(shifted(h2, e), x2))
    place = 10
    for distance, base in MERGES:
        latter = (vturn(head, -distance), vturn(tail, -distance))
        inner_tail, inner_head, head, tail = merge_rhs(fac_ref, base, (head, tail), latter)
        keep_vector(val_ref, place, inner_tail)
        keep_vector(val_ref, place + 5, inner_head)
        place += 10
    keep_vector(val_ref, place, mv(block(fac_ref, CLOSE), head))
    own = vminus(tail, mv(block(fac_ref, CLOSE + 50), head))
    nxt = vturn([-value for value in mv(block(fac_ref, CLOSE + 75), head)], -WIDTH)
    for distance, base in STAGES:
        place += 5
        value, own, nxt = stage_rhs(fac_ref, base, own, nxt, distance)
        keep_vector(val_ref, place, value)
    end_ref[...] = jnp.zeros_like(end_ref)
    keep_vector(end_ref, 3, own)
    keep_vector(end_ref, 8, nxt)
    pack_ref[:112, :] = part_ref[:112, :]
    row = lax.broadcasted_iota(jnp.int32, (8, LANES), 0)
    pack_ref[112:120, :] = jnp.where(row < 3, part_ref[112:120, :], rows_of_last(end_ref, 0))
    pack_ref[120:125, :] = rows_of_last(end_ref, 1)[:5]


def solve_kernel(sent_ref, jac_ref, step_ref, fac_ref, val_ref, out_ref, all_ref, red_ref, x_ref, w_ref):
    e = damping
    for device in range(16):
        all_ref[ROWS * device : ROWS * device + SENT, :] = sent_ref[device]
    row = lax.broadcasted_iota(jnp.int32, (CHUNKS, LANES), 0)

    def packed(parity, number):
        return all_ref[pl.ds(parity * ROWS + number, 8, stride=2 * ROWS), :]

    def packed_block(parity, base):
        return [[packed(parity, base + 5 * a + b) for b in N] for a in N]

    def packed_vector(parity, base):
        return [packed(parity, base + a) for a in N]

    def packed_symmetric(parity, base):
        result = [[None] * 5 for _ in N]
        for a in N:
            for b in range(a, 5):
                result[a][b] = result[b][a] = packed(parity, base)
                base += 1
        return result

    m_even = packed_symmetric(0, 100)
    m_odd = packed_symmetric(1, 100)
    value, (vlow, vupp) = solved(
        plus(packed_block(0, 25), mm(packed_block(1, 50), m_even)),
        vplus(packed_vector(0, 115), packed_vector(1, 120)),
        packed_block(0, 0),
        packed_block(1, 75),
    )
    keep(red_ref, VLOW, vlow)
    keep(red_ref, VUPP, vupp)
    keep_vector(x_ref, 4, value)
    cross = mm(packed_block(1, 0), m_even)
    own = minus(packed_block(1, 25), mm(cross, vupp))
    low = negative(mm(cross, vlow))
    own_rhs = vminus(packed_vector(1, 115), mv(cross, value))
    back = packed_block(0, 75)
    nxt = minus(packed_block(0, 50), mm(back, vlow))
    upp = negative(mm(back, vupp))
    nxt_rhs = vminus(packed_vector(0, 120), mv(back, value))
    first, last = row == 0, row == CHUNKS - 1
    low = mm(low, mturn(m_odd, 1))
    low = [[jnp.where(first, 0.0, low[a][b]) for b in N] for a in N]
    nxt = mm(mturn(nxt, -1), m_odd)
    nxt = [[jnp.where(last, 0.0, nxt[a][b]) for b in N] for a in N]
    upp = [[jnp.where(last, 0.0, turn(upp[a][b], -1)) for b in N] for a in N]
    nxt_rhs = [jnp.where(last, 0.0, turn(nxt_rhs[a], -1)) for a in N]
    for distance in (1, 2, 4):
        value, (vlow, vupp) = solved(plus(own, nxt), vplus(own_rhs, nxt_rhs), low, upp)
        own_rhs = vminus(own_rhs, mv(low, vturn(value, distance)))
        nxt_rhs = vminus(nxt_rhs, mv(upp, vturn(value, -distance)))
        low, own, nxt, upp = next_rows(low, own, nxt, upp, vlow, vupp, distance)
    x = solved(plus(own, nxt), vplus(own_rhs, nxt_rhs))[0]
    w_odd = mv(m_odd, x)
    before = [jnp.where(first, 0.0, turn(w_odd[a], 1)) for a in N]
    x_even = stage_back(red_ref, 0, vector(x_ref, 4), before, x)
    w_even = mv(m_even, x_even)
    position = lax.axis_index("line")
    half, odd = position // 2, position % 2
    is_odd = odd == 1
    for a in N:
        w_ref[8 * a : 8 * a + 8, :] = jnp.where(is_odd, w_even[a], before[a])
        x_ref[8 * a : 8 * a + 8, :] = jnp.where(is_odd, x[a], x_even[a])
    ends = [jnp.broadcast_to(x_ref[pl.ds(8 * a + half, 1), :], (CHUNKS, LANES)) for a in N]
    w = [jnp.broadcast_to(w_ref[pl.ds(8 * a + half, 1), :], (CHUNKS, LANES)) for a in N]

    def neighbour(values, distance):
        return [jnp.where(row < distance, w[a], turn(values[a], distance)) for a in N]

    last = ends
    place = VALUES - 5
    for distance, base in reversed(STAGES):
        found = stage_back(fac_ref, base, vector(val_ref, place), neighbour(last, distance), vturn(last, -distance))
        place -= 5
        chosen = (row % (2 * distance)) == distance - WIDTH
        last = [jnp.where(chosen, found[a], last[a]) for a in N]
    if STAGES:
        w = mv(shifted(half_before(half_jacobian(jac_ref, 3)), e), neighbour(last, WIDTH))
    first = vplus(
        vector(val_ref, place), vminus(mv(block(fac_ref, CLOSE), w), mv(block(fac_ref, CLOSE + 25), last))
    )
    for distance, base in reversed(MERGES):
        place -= 10
        tail, head = merge_back(fac_ref, base, vector(val_ref, place), vector(val_ref, place + 5), first, last)
        latter = (row % (2 * distance)) >= distance
        first = [jnp.where(latter, turn(head[a], distance), first[a]) for a in N]
        last = [jnp.where(latter, turn(last[a], distance), tail[a]) for a in N]
    d1 = diagonal(step_ref, 1)
    d2 = diagonal(step_ref, 2)
    part = mv(block(fac_ref, 25), first)
    x1 = vplus(vplus(vector(val_ref, 0), [d2 * value for value in part]), mv(block(fac_ref, 50), last))
    far = mv(block(fac_ref, 75), last)
    near = mv(shifted(half_jacobian(jac_ref, 1), e), part)
    x2 = vplus(vector(val_ref, 5), vminus(near, [d1 * value for value in far]))
    for a in N:
        out_ref[a, pl.ds(0, CHUNKS, stride=CELLS), :] = first[a]
        out_ref[a, pl.ds(1, CHUNKS, stride=CELLS), :] = x1[a]
        out_ref[a, pl.ds(2, CHUNKS, stride=CELLS), :] = x2[a]
        out_ref[a, pl.ds(3, CHUNKS, stride=CELLS), :] = last[a]


INTERPRET = False


VMEM = pl.BlockSpec(memory_space=pltpu.VMEM)
HBM = pl.BlockSpec(memory_space=pltpu.MemorySpace.HBM)


def kept(shape, dtype=jnp.float32):
    return jax.ShapeDtypeStruct(shape, dtype) if INTERPRET else pltpu.VMEM(shape, dtype)


def inside(values):
    return values if INTERPRET else [pltpu.with_memory_space_constraint(value, pltpu.VMEM) for value in values]


def outside(values):
    return values if INTERPRET else [pltpu.with_memory_space_constraint(value, pltpu.MemorySpace.HBM) for value in values]


def run(kernel, name, outs, args, scratch, far_args=0, far_outs=0):
    return pl.pallas_call(
        kernel,
        out_shape=outs,
        in_specs=[HBM] * far_args + [VMEM] * (len(args) - far_args),
        out_specs=[HBM] * far_outs + [VMEM] * (len(outs) - far_outs),
        scratch_shapes=scratch,
        compiler_params=pltpu.CompilerParams(vmem_limit_bytes=12 << 20),
        interpret=INTERPRET,
        name=name,
    )(*outside(args[:far_args]), *inside(args[far_args:]))


def tiles(count):
    return pltpu.VMEM((8 * count, LANES), jnp.float32)


def shards(jacobian, time_step, source, cross_flux):
    count = lax.axis_size("cross")
    cells = CHUNKS * CELLS
    even_swap, odd_swap = (
        lax.ppermute(
            cross_flux,
            "cross",
            [pair for i in range(start, count - 1, 2) for pair in ((i, i + 1), (i + 1, i))],
        )
        for start in (0, 1)
    )
    jac, step, src, flux, factors, part = run(
        factor_kernel,
        "factor",
        [
            kept((5, 5, cells, LANES)),
            kept((cells, LANES)),
            kept((5, cells, LANES), jnp.bfloat16),
            kept((5, cells, LANES), jnp.bfloat16),
            kept((8 * TILES, LANES)),
            kept((120, LANES)),
        ],
        [jacobian, time_step, source, cross_flux],
        [tiles(120), pltpu.SemaphoreType.DMA((8,))],
        far_args=4,
    )
    packet, values = run(
        rhs_kernel,
        "right_side",
        [kept((SENT, LANES)), kept((8 * VALUES, LANES))],
        [jac, step, src, flux, even_swap, odd_swap, factors, part],
        [pltpu.VMEM((5, cells, LANES), jnp.float32), tiles(16)],
    )
    packets = lax.all_gather(packet, "line", axis=0)
    return run(
        solve_kernel,
        "solve",
        [kept((5, cells, LANES))],
        [packets, jac, step, factors, values],
        [
            tiles(2 * ROWS),
            tiles(STAGE),
            tiles(16),
            tiles(5),
        ],
    )[0]


def solution(mesh):
    placed = (
        P(None, None, "line", "cross"),
        P("line", "cross"),
        P(None, "line", "cross"),
        P(None, "line", "cross"),
    )
    return jax.shard_map(
        shards, mesh=mesh, in_specs=placed, out_specs=P(None, "line", "cross"), check_vma=False
    )
```

```python
import jax
import jax.numpy as jnp
from jax import lax
from jax.experimental import pallas as pl
from jax.experimental.pallas import tpu as pltpu
from jax.sharding import PartitionSpec as P

NZ = 8
damping = 0.05

CHUNKS = 8
CELLS = 4
LANES = 128
SENT = 125
ROWS = 128
INV, LOW, UPP, VLOW, VUPP = (25 * k for k in range(5))
STAGE = 125
N = range(5)


def tile(ref, number):
    return ref[8 * number : 8 * number + 8, :]


def block(ref, base):
    return [[tile(ref, base + 5 * a + b) for b in N] for a in N]


def vector(ref, base):
    return [tile(ref, base + a) for a in N]


def keep(ref, base, matrix):
    for a in N:
        for b in N:
            ref[8 * (base + 5 * a + b) : 8 * (base + 5 * a + b) + 8, :] = matrix[a][b]


def keep_vector(ref, base, values):
    for a in N:
        ref[8 * (base + a) : 8 * (base + a) + 8, :] = values[a]


def total(terms):
    result = terms[0]
    for term in terms[1:]:
        result = result + term
    return result


def mm(left, right):
    return [[total([left[a][k] * right[k][b] for k in N]) for b in N] for a in N]


def mv(left, right):
    return [total([left[a][k] * right[k] for k in N]) for a in N]


def plus(left, right):
    return [[left[a][b] + right[a][b] for b in N] for a in N]


def minus(left, right):
    return [[left[a][b] - right[a][b] for b in N] for a in N]


def negative(matrix):
    return [[-matrix[a][b] for b in N] for a in N]


def vplus(left, right):
    return [left[a] + right[a] for a in N]


def vminus(left, right):
    return [left[a] - right[a] for a in N]


def scaled(factor, matrix):
    return [[factor * matrix[a][b] for b in N] for a in N]


def shifted(matrix, amount):
    return [[matrix[a][b] + amount if a == b else matrix[a][b] for b in N] for a in N]


def turn(value, count):
    return pltpu.roll(value, count % CHUNKS, axis=0)


def flipped(matrix):
    return [[matrix[b][a] for b in N] for a in N]


def mturn(matrix, count):
    return [[turn(matrix[a][b], count) for b in N] for a in N]


def vturn(values, count):
    return [turn(values[a], count) for a in N]


def inverse_and_solved(matrix, *sides):
    m = [list(row) + [side[a][b] for side in sides for b in N] for a, row in enumerate(matrix)]
    width = len(m[0])
    for k in N:
        pivot = 1.0 / m[k][k]
        for b in range(width):
            m[k][b] = pivot if b == k else m[k][b] * pivot
        for a in N:
            if a != k:
                factor = m[a][k]
                for b in range(width):
                    m[a][b] = -factor * pivot if b == k else m[a][b] - factor * m[k][b]
    return [[row[at : at + 5] for row in m] for at in range(0, width, 5)]


def solved(matrix, values, *sides):
    m = [list(row) + [values[a]] + [side[a][b] for side in sides for b in N] for a, row in enumerate(matrix)]
    width = len(m[0])
    for k in N:
        pivot = 1.0 / m[k][k]
        for b in range(k + 1, width):
            m[k][b] = m[k][b] * pivot
        for a in N:
            if a != k:
                for b in range(k + 1, width):
                    m[a][b] = m[a][b] - m[a][k] * m[k][b]
    return [row[5] for row in m], [[row[at : at + 5] for row in m] for at in range(6, width, 5)]


def half_jacobian(jac_ref, cell):
    half = [[None] * 5 for _ in N]
    for a in N:
        for b in range(a, 5):
            half[a][b] = half[b][a] = 0.5 * jac_ref[a, b, pl.ds(cell, CHUNKS, stride=CELLS), :]
    return half


def half_before(half_last):
    first = lax.broadcasted_iota(jnp.int32, (CHUNKS, LANES), 0) == 0
    result = [[None] * 5 for _ in N]
    for a in N:
        for b in range(a, 5):
            outside = 1.0 - damping if a == b else 0.0
            result[a][b] = result[b][a] = jnp.where(first, outside, turn(half_last[a][b], 1))
    return result


def diagonal(step_ref, cell):
    return 1.0 / step_ref[pl.ds(cell, CHUNKS, stride=CELLS), :] + 2.0 * damping


def next_rows(low, own, nxt, upp, vlow, vupp, distance):
    vlow_before, vupp_before = mturn(vlow, distance), mturn(vupp, distance)
    vlow_after, vupp_after = vlow_before, vupp_before
    if 2 * distance != CHUNKS:
        vlow_after, vupp_after = mturn(vlow, -distance), mturn(vupp, -distance)
    return (
        mm(low, vlow_before),
        minus(own, mm(low, vupp_before)),
        minus(nxt, mm(upp, vlow_after)),
        mm(upp, vupp_after),
    )


def stage(fac_ref, base, low, own, nxt, upp, distance):
    inv, vlow, vupp = inverse_and_solved(plus(own, nxt), low, upp)
    keep(fac_ref, base + INV, inv)
    keep(fac_ref, base + LOW, low)
    keep(fac_ref, base + UPP, upp)
    keep(fac_ref, base + VLOW, vlow)
    keep(fac_ref, base + VUPP, vupp)
    low, own, nxt, upp = next_rows(low, own, nxt, upp, vlow, vupp, distance)
    return negative(low), own, nxt, negative(upp)


def stage_rhs(fac_ref, base, own, nxt, distance):
    value = mv(block(fac_ref, base + INV), vplus(own, nxt))
    own = vminus(own, mv(block(fac_ref, base + LOW), vturn(value, distance)))
    nxt = vminus(nxt, mv(block(fac_ref, base + UPP), vturn(value, -distance)))
    return value, own, nxt


def stage_back(fac_ref, base, value, before, after):
    return vminus(
        vminus(value, mv(block(fac_ref, base + VLOW), before)), mv(block(fac_ref, base + VUPP), after)
    )


def merge(fac_ref, base, former, latter, upp, low):
    head_head, head_tail, tail_head, tail_tail = former
    inv_head, carry, reach = inverse_and_solved(latter[0], low, latter[1])
    inv_tail, tail_by_head, tail_by_tail = inverse_and_solved(
        plus(tail_tail, mm(upp, carry)), tail_head, mm(upp, reach)
    )
    head_by_head = mm(carry, tail_by_head)
    head_by_tail = minus(reach, mm(carry, tail_by_tail))
    for number, kept in enumerate(
        (
            inv_head,
            carry,
            inv_tail,
            upp,
            head_tail,
            latter[2],
            tail_by_head,
            tail_by_tail,
            head_by_head,
            head_by_tail,
        )
    ):
        keep(fac_ref, base + 25 * number, kept)
    return (
        minus(head_head, mm(head_tail, tail_by_head)),
        mm(head_tail, tail_by_tail),
        negative(mm(latter[2], head_by_head)),
        minus(latter[3], mm(latter[2], head_by_tail)),
    )


def merge_rhs(fac_ref, base, former, latter):
    head = mv(block(fac_ref, base), latter[0])
    tail = mv(block(fac_ref, base + 50), vminus(former[1], mv(block(fac_ref, base + 75), head)))
    head = vplus(head, mv(block(fac_ref, base + 25), tail))
    return (
        tail,
        head,
        vminus(former[0], mv(block(fac_ref, base + 100), tail)),
        vminus(latter[1], mv(block(fac_ref, base + 125), head)),
    )


def merge_back(fac_ref, base, tail, head, first, last):
    tail = vplus(
        vminus(tail, mv(block(fac_ref, base + 150), first)), mv(block(fac_ref, base + 175), last)
    )
    head = vminus(
        vminus(head, mv(block(fac_ref, base + 200), first)), mv(block(fac_ref, base + 225), last)
    )
    return tail, head


def rows_of_last(ref, group):
    return ref[pl.ds(64 * group + CHUNKS - WIDTH, 8, stride=8), :]


WIDTH = 2
MERGES = tuple((1 << k, 100 + 250 * k) for k in range(WIDTH.bit_length() - 1))
CLOSE = 100 + 250 * len(MERGES)
STAGES = tuple((WIDTH << k, CLOSE + 100 + 125 * k) for k in range((CHUNKS // WIDTH).bit_length() - 1))
TILES = CLOSE + 100 + 125 * len(STAGES)
VALUES = 15 + 10 * len(MERGES) + 5 * len(STAGES)


def factor_kernel(
    jac_hbm, step_hbm, src_hbm, flux_hbm, jac_ref, step_ref, src_ref, flux_ref, fac_ref, pack_ref, end_ref, sems
):
    needed = [pltpu.make_async_copy(jac_hbm.at[a, a:], jac_ref.at[a, a:], sems.at[a]) for a in N]
    needed.append(pltpu.make_async_copy(step_hbm, step_ref, sems.at[5]))
    later = [
        pltpu.make_async_copy(src_hbm, src_ref, sems.at[6]),
        pltpu.make_async_copy(flux_hbm, flux_ref, sems.at[7]),
    ]
    for copy in needed + later:
        copy.start()
    for copy in needed:
        copy.wait()
    factor(jac_ref, step_ref, fac_ref, pack_ref, end_ref)
    for copy in later:
        copy.wait()


def factor(jac_ref, step_ref, fac_ref, pack_ref, end_ref):
    e = damping
    h0 = half_jacobian(jac_ref, 0)
    h1 = half_jacobian(jac_ref, 1)
    h2 = half_jacobian(jac_ref, 2)
    h3 = half_jacobian(jac_ref, 3)
    d1 = diagonal(step_ref, 1)
    d2 = diagonal(step_ref, 2)
    h0p, h1p, h2p, h3p = shifted(h0, e), shifted(h1, e), shifted(h2, e), shifted(h3, e)
    h0m, h1m, h2m, h3m = shifted(h0, -e), shifted(h1, -e), shifted(h2, -e), shifted(h3, -e)
    inv, by_low, by_upp = inverse_and_solved(shifted(mm(h2m, h1p), d1 * d2), h0p, mm(h2m, h3m))
    by_end = mm(flipped(inv), h3m)
    pair = mm(h2p, h1p)
    group = (
        shifted(mm(h1m, scaled(d2, by_low)), diagonal(step_ref, 0)),
        mm(h1m, by_upp),
        negative(mm(pair, by_low)),
        shifted(mm(scaled(d1, h2p), by_end), diagonal(step_ref, 3)),
    )
    keep(fac_ref, 0, inv)
    keep(fac_ref, 25, by_low)
    keep(fac_ref, 50, by_upp)
    keep(fac_ref, 75, by_end)
    for distance, base in MERGES:
        latter = tuple(mturn(part, -distance) for part in group)
        group = merge(fac_ref, base, group, latter, mturn(h0m, -distance), mturn(h3p, 1 - distance))
    head_head, head_tail, tail_head, tail_tail = group
    inv, reach = inverse_and_solved(head_head, head_tail)
    through = mm(tail_head, inv)
    into = mm(h0m, inv)
    keep(fac_ref, CLOSE, inv)
    keep(fac_ref, CLOSE + 25, reach)
    keep(fac_ref, CLOSE + 50, through)
    keep(fac_ref, CLOSE + 75, into)
    own = minus(tail_tail, mm(tail_head, reach))
    upp = mturn(negative(mm(h0m, reach)), -WIDTH)
    low, nxt = through, into
    if STAGES:
        link = shifted(half_before(h3), e)
        low, nxt = mm(through, link), mm(into, link)
    nxt = mturn(nxt, -WIDTH)
    for distance, base in STAGES:
        low, own, nxt, upp = stage(fac_ref, base, low, own, nxt, upp, distance)
    keep(end_ref, 0, low)
    keep(end_ref, 25, own)
    keep(end_ref, 50, nxt)
    keep(end_ref, 75, upp)
    place = 100
    for a in N:
        for b in range(a, 5):
            end_ref[8 * place : 8 * place + 8, :] = turn(h3p[a][b], 1 - WIDTH)
            place += 1
    for number in range(15):
        pack_ref[8 * number : 8 * number + 8, :] = rows_of_last(end_ref, number)


def rhs_kernel(
    jac_ref, step_ref, src_ref, flux_ref, even_ref, odd_ref, fac_ref, part_ref, pack_ref, val_ref, res_ref, end_ref
):
    e = damping
    lane = lax.broadcasted_iota(jnp.int32, (CHUNKS * CELLS, LANES), 1)
    is_even = lax.axis_index("cross") % 2 == 0
    for a in N:
        flux = flux_ref[a].astype(jnp.float32)
        even_swap = even_ref[a].astype(jnp.float32)
        odd_swap = odd_ref[a].astype(jnp.float32)
        after = jnp.where(is_even, even_swap, odd_swap)
        before = jnp.where(is_even, odd_swap, even_swap)
        upper = pltpu.roll(jnp.where(lane < NZ, after, flux), LANES - NZ, axis=1)
        lower = pltpu.roll(jnp.where(lane >= LANES - NZ, before, flux), NZ, axis=1)
        res_ref[a] = src_ref[a].astype(jnp.float32) - 0.5 * (upper - lower)
    r0, r1, r2, r3 = ([res_ref[a, pl.ds(cell, CHUNKS, stride=CELLS), :] for a in N] for cell in range(CELLS))
    h1 = half_jacobian(jac_ref, 1)
    h2 = half_jacobian(jac_ref, 2)
    d1 = diagonal(step_ref, 1)
    d2 = diagonal(step_ref, 2)
    inv = block(fac_ref, 0)
    part = mv(inv, r1)
    x1 = vminus([d2 * value for value in part], mv(inv, mv(shifted(h2, -e), r2)))
    x2 = vplus(mv(shifted(h1, e), part), [d1 * value for value in mv(flipped(inv), r2)])
    keep_vector(val_ref, 0, x1)
    keep_vector(val_ref, 5, x2)
    head = vminus(r0, mv(shifted(h1, -e), x1))
    tail = vplus(r3, mv(shifted(h2, e), x2))
    place = 10
    for distance, base in MERGES:
        latter = (vturn(head, -distance), vturn(tail, -distance))
        inner_tail, inner_head, head, tail = merge_rhs(fac_ref, base, (head, tail), latter)
        keep_vector(val_ref, place, inner_tail)
        keep_vector(val_ref, place + 5, inner_head)
        place += 10
    keep_vector(val_ref, place, mv(block(fac_ref, CLOSE), head))
    own = vminus(tail, mv(block(fac_ref, CLOSE + 50), head))
    nxt = vturn([-value for value in mv(block(fac_ref, CLOSE + 75), head)], -WIDTH)
    for distance, base in STAGES:
        place += 5
        value, own, nxt = stage_rhs(fac_ref, base, own, nxt, distance)
        keep_vector(val_ref, place, value)
    end_ref[...] = jnp.zeros_like(end_ref)
    keep_vector(end_ref, 3, own)
    keep_vector(end_ref, 8, nxt)
    pack_ref[:112, :] = part_ref[:112, :]
    row = lax.broadcasted_iota(jnp.int32, (8, LANES), 0)
    pack_ref[112:120, :] = jnp.where(row < 3, part_ref[112:120, :], rows_of_last(end_ref, 0))
    pack_ref[120:125, :] = rows_of_last(end_ref, 1)[:5]


def solve_kernel(sent_ref, jac_ref, step_ref, fac_ref, val_ref, out_ref, all_ref, red_ref, x_ref, w_ref):
    e = damping
    for device in range(16):
        all_ref[ROWS * device : ROWS * device + SENT, :] = sent_ref[device]
    row = lax.broadcasted_iota(jnp.int32, (CHUNKS, LANES), 0)

    def packed(parity, number):
        return all_ref[pl.ds(parity * ROWS + number, 8, stride=2 * ROWS), :]

    def packed_block(parity, base):
        return [[packed(parity, base + 5 * a + b) for b in N] for a in N]

    def packed_vector(parity, base):
        return [packed(parity, base + a) for a in N]

    def packed_symmetric(parity, base):
        result = [[None] * 5 for _ in N]
        for a in N:
            for b in range(a, 5):
                result[a][b] = result[b][a] = packed(parity, base)
                base += 1
        return result

    m_even = packed_symmetric(0, 100)
    m_odd = packed_symmetric(1, 100)
    value, (vlow, vupp) = solved(
        plus(packed_block(0, 25), mm(packed_block(1, 50), m_even)),
        vplus(packed_vector(0, 115), packed_vector(1, 120)),
        packed_block(0, 0),
        packed_block(1, 75),
    )
    keep(red_ref, VLOW, vlow)
    keep(red_ref, VUPP, vupp)
    keep_vector(x_ref, 4, value)
    cross = mm(packed_block(1, 0), m_even)
    own = minus(packed_block(1, 25), mm(cross, vupp))
    low = mm(cross, vlow)
    own_rhs = vminus(packed_vector(1, 115), mv(cross, value))
    back = packed_block(0, 75)
    nxt = minus(packed_block(0, 50), mm(back, vlow))
    upp = mm(back, vupp)
    nxt_rhs = vminus(packed_vector(0, 120), mv(back, value))
    first, last = row == 0, row == CHUNKS - 1
    low = mm(low, mturn(m_odd, 1))
    low = [[jnp.where(first, 0.0, low[a][b]) for b in N] for a in N]
    nxt = mm(mturn(nxt, -1), m_odd)
    nxt = [[jnp.where(last, 0.0, nxt[a][b]) for b in N] for a in N]
    upp = [[jnp.where(last, 0.0, turn(upp[a][b], -1)) for b in N] for a in N]
    nxt_rhs = [jnp.where(last, 0.0, turn(nxt_rhs[a], -1)) for a in N]
    for distance in (1, 2, 4):
        value, (vlow, vupp) = solved(plus(own, nxt), vplus(own_rhs, nxt_rhs), low, upp)
        own_rhs = vplus(own_rhs, mv(low, vturn(value, distance)))
        nxt_rhs = vplus(nxt_rhs, mv(upp, vturn(value, -distance)))
        low, own, nxt, upp = next_rows(low, own, nxt, upp, vlow, vupp, distance)
    x = solved(plus(own, nxt), vplus(own_rhs, nxt_rhs))[0]
    w_odd = mv(m_odd, x)
    before = [jnp.where(first, 0.0, turn(w_odd[a], 1)) for a in N]
    x_even = stage_back(red_ref, 0, vector(x_ref, 4), before, x)
    w_even = mv(m_even, x_even)
    position = lax.axis_index("line")
    half, odd = position // 2, position % 2
    is_odd = odd == 1
    for a in N:
        w_ref[8 * a : 8 * a + 8, :] = jnp.where(is_odd, w_even[a], before[a])
        x_ref[8 * a : 8 * a + 8, :] = jnp.where(is_odd, x[a], x_even[a])
    ends = [jnp.broadcast_to(x_ref[pl.ds(8 * a + half, 1), :], (CHUNKS, LANES)) for a in N]
    w = [jnp.broadcast_to(w_ref[pl.ds(8 * a + half, 1), :], (CHUNKS, LANES)) for a in N]

    def neighbour(values, distance):
        return [jnp.where(row < distance, w[a], turn(values[a], distance)) for a in N]

    last = ends
    place = VALUES - 5
    for distance, base in reversed(STAGES):
        found = stage_back(fac_ref, base, vector(val_ref, place), neighbour(last, distance), vturn(last, -distance))
        place -= 5
        chosen = (row % (2 * distance)) == distance - WIDTH
        last = [jnp.where(chosen, found[a], last[a]) for a in N]
    if STAGES:
        w = mv(shifted(half_before(half_jacobian(jac_ref, 3)), e), neighbour(last, WIDTH))
    first = vplus(
        vector(val_ref, place), vminus(mv(block(fac_ref, CLOSE), w), mv(block(fac_ref, CLOSE + 25), last))
    )
    for distance, base in reversed(MERGES):
        place -= 10
        tail, head = merge_back(fac_ref, base, vector(val_ref, place), vector(val_ref, place + 5), first, last)
        latter = (row % (2 * distance)) >= distance
        first = [jnp.where(latter, turn(head[a], distance), first[a]) for a in N]
        last = [jnp.where(latter, turn(last[a], distance), tail[a]) for a in N]
    d1 = diagonal(step_ref, 1)
    d2 = diagonal(step_ref, 2)
    part = mv(block(fac_ref, 25), first)
    x1 = vplus(vplus(vector(val_ref, 0), [d2 * value for value in part]), mv(block(fac_ref, 50), last))
    far = mv(block(fac_ref, 75), last)
    near = mv(shifted(half_jacobian(jac_ref, 1), e), part)
    x2 = vplus(vector(val_ref, 5), vminus(near, [d1 * value for value in far]))
    for a in N:
        out_ref[a, pl.ds(0, CHUNKS, stride=CELLS), :] = first[a]
        out_ref[a, pl.ds(1, CHUNKS, stride=CELLS), :] = x1[a]
        out_ref[a, pl.ds(2, CHUNKS, stride=CELLS), :] = x2[a]
        out_ref[a, pl.ds(3, CHUNKS, stride=CELLS), :] = last[a]


INTERPRET = False


VMEM = pl.BlockSpec(memory_space=pltpu.VMEM)
HBM = pl.BlockSpec(memory_space=pltpu.MemorySpace.HBM)


def kept(shape, dtype=jnp.float32):
    return jax.ShapeDtypeStruct(shape, dtype) if INTERPRET else pltpu.VMEM(shape, dtype)


def inside(values):
    return values if INTERPRET else [pltpu.with_memory_space_constraint(value, pltpu.VMEM) for value in values]


def outside(values):
    return values if INTERPRET else [pltpu.with_memory_space_constraint(value, pltpu.MemorySpace.HBM) for value in values]


def run(kernel, name, outs, args, scratch, far_args=0, far_outs=0):
    return pl.pallas_call(
        kernel,
        out_shape=outs,
        in_specs=[HBM] * far_args + [VMEM] * (len(args) - far_args),
        out_specs=[HBM] * far_outs + [VMEM] * (len(outs) - far_outs),
        scratch_shapes=scratch,
        compiler_params=pltpu.CompilerParams(vmem_limit_bytes=12 << 20),
        interpret=INTERPRET,
        name=name,
    )(*outside(args[:far_args]), *inside(args[far_args:]))


def tiles(count):
    return pltpu.VMEM((8 * count, LANES), jnp.float32)


def shards(jacobian, time_step, source, cross_flux):
    count = lax.axis_size("cross")
    cells = CHUNKS * CELLS
    even_swap, odd_swap = (
        lax.ppermute(
            cross_flux,
            "cross",
            [pair for i in range(start, count - 1, 2) for pair in ((i, i + 1), (i + 1, i))],
        )
        for start in (0, 1)
    )
    jac, step, src, flux, factors, part = run(
        factor_kernel,
        "factor",
        [
            kept((5, 5, cells, LANES)),
            kept((cells, LANES)),
            kept((5, cells, LANES), jnp.bfloat16),
            kept((5, cells, LANES), jnp.bfloat16),
            kept((8 * TILES, LANES)),
            kept((120, LANES)),
        ],
        [jacobian, time_step, source, cross_flux],
        [tiles(120), pltpu.SemaphoreType.DMA((8,))],
        far_args=4,
    )
    packet, values = run(
        rhs_kernel,
        "right_side",
        [kept((SENT, LANES)), kept((8 * VALUES, LANES))],
        [jac, step, src, flux, even_swap, odd_swap, factors, part],
        [pltpu.VMEM((5, cells, LANES), jnp.float32), tiles(16)],
    )
    packets = lax.all_gather(packet, "line", axis=0)
    return run(
        solve_kernel,
        "solve",
        [kept((5, cells, LANES))],
        [packets, jac, step, factors, values],
        [
            tiles(2 * ROWS),
            tiles(STAGE),
            tiles(16),
            tiles(5),
        ],
    )[0]


def solution(mesh):
    placed = (
        P(None, None, "line", "cross"),
        P("line", "cross"),
        P(None, "line", "cross"),
        P(None, "line", "cross"),
    )
    return jax.shard_map(
        shards, mesh=mesh, in_specs=placed, out_specs=P(None, "line", "cross"), check_vma=False
    )
```
